32 devices in a mesh: groups: 2 (over x), space: 16 (over z, y, core).
Axes of the slice: x: 2, y: 2, z: 4, core: 2. Of those that a mesh axis runs over, the one named last changes fastest.
Arguments:
- slowness: float32 [512, 4096], P(('groups', 'space')), parts along dimension 0, may hold values from 0.25 to 1
- ocean: int32 [512, 4096], P(('groups', 'space')), parts along dimension 0, may hold values 0 or 1
- start_times: float32 [8, 256, 4096], P('groups', 'space'), parts along dimension 0, may hold values from 0 to 96
- source_cells: int32 [8], P('groups'), parts along dimension 0, may hold values from 0 to 1048575
- gauge_cells: int32 [4096], P(('groups', 'space')), parts along dimension 0, may hold values from 0 to 65535
- gauge_owner: int32 [4096, 1], P(('groups', 'space')), parts along dimension 0, may hold values from 0 to 15; in each aligned block of 128 rows (0 to 127, 128 to 255, ...) at most 16 rows name the same one
Outputs:
- arrival: float32 [512, 4096], P(('groups', 'space')), parts along dimension 0
- gauge_arrivals: float32 [32, 4, 256], P(('groups', 'space')), parts along dimension 0
The draws below stay inside these ranges and needn't reach their ends.
There are 2 independent parts, one for each index of `groups`. The reference program is written for one: setup_inputs(seed, part) draws one part's arguments, and reference() takes and returns one part's arrays. A program takes and returns all parts, laid end to end along the dimension named above; each array names one. Nothing has to cross between parts.
Inputs may be any that keep to these rules, and one draw needn't show every extreme that they name: `gauge_owner`: among the 128 gauges of one device block, no owner is named more than 16 times, a bound that some block reaches.
All inputs are finite; a program needn't handle non-finite values. No bound on the sum of `ocean` on one device may be relied on, other than what follows from the above.
Results may differ from the reference program's by a relative error of at most 0.00016.
Values sent between devices are 32-bit elements; how exact they have to be, the bound alone decides.
No kernel may reach another device: no remote copies, remote signals or barrier semaphores. Data moves between devices by JAX's collectives and lax.ppermute only.
A program may use at most 128 MiB of HBM per device.

```python
import math
import jax
import jax.numpy as jnp
import numpy as np
from jax import lax

R_DEV = 16
W = 4096
SOURCES = 4
SWEEPS = 8
BLOCKS = 3
G_DEV = 128
NROWS = 256
GAUGES = 2048
CAP = 16
N_SPACE = 16


def draw_start_times(key, part):
    key_list = jax.random.split(jax.random.fold_in(key, 7), 7)
    sweep_total = BLOCKS * SWEEPS
    row_frac = jnp.arange(NROWS, dtype=jnp.float32)[None, :, None] / NROWS
    col_frac = jnp.arange(W, dtype=jnp.float32)[None, None, :] / W
    wave_rows = jax.random.randint(key_list[0], (SOURCES, 1, 1), 1, 5).astype(jnp.float32)
    wave_cols = jax.random.randint(key_list[1], (SOURCES, 1, 1), 1, 5).astype(jnp.float32)
    phase_rows = jax.random.uniform(key_list[2], (SOURCES, 1, 1), jnp.float32)
    phase_cols = jax.random.uniform(key_list[3], (SOURCES, 1, 1), jnp.float32)
    smooth = 0.5 + 0.5 * jnp.sin(2.0 * math.pi * (wave_rows * row_frac + phase_rows)) * jnp.cos(2.0 * math.pi * (wave_cols * col_frac + phase_cols))
    grid_shape = (SOURCES, NROWS, W)
    rough_part = jax.random.uniform(key_list[4], grid_shape, jnp.float32)
    seeded = jax.random.randint(key_list[5], grid_shape, 0, 4 * sweep_total * sweep_total) == 0
    seed_value = jax.random.uniform(key_list[6], grid_shape, jnp.float32)
    ceiling = 20.0 + 50.0 * smooth + 6.0 * rough_part
    lowest = 6.0 * seed_value
    return jnp.where(seeded, lowest, ceiling).astype(jnp.float32)


def set_ends(entries, rng, least, largest):
    longest = entries.shape.index(max(entries.shape))
    spots = []
    for shift in (0, 1):
        where = [jax.random.randint(jax.random.fold_in(rng, axis), (), 0, length) for axis, length in enumerate(entries.shape)]
        where[longest] = (where[longest] + shift) % entries.shape[longest]
        spots.append(tuple(where))
    return entries.at[spots[0]].set(least).at[spots[1]].set(largest)


def block_levels(rng, dims, cuts, least, high):
    def one(dim, shards_of):
        steps = jax.random.uniform(jax.random.fold_in(jax.random.fold_in(rng, 6), dim), (shards_of,), jnp.float32, least / len(cuts), high / len(cuts))
        return jnp.repeat(jnp.exp(steps), dims[dim] // shards_of).reshape((-1,) + (1,) * (len(dims) - dim - 1))

    loudness = one(*cuts[0])
    for cut in cuts[1:]:
        loudness = loudness * one(*cut)
    return loudness


def routed_block(key, own, number, rows, count, top, most, lean):
    sequence = jax.random.permutation(key, count)
    crowded, usual = load_shares(count, rows * top, most, lean, True), load_shares(count, rows * top, most, lean, False)
    places = jnp.arange(count)

    def named(sizes, offset_by):
        used = int((sizes > 0).sum())
        fixed = max(1, used // 4)
        moved = fixed + (places - fixed + offset_by * (used - fixed)) % max(1, count - fixed)
        return jnp.zeros((count,), jnp.int32).at[sequence[jnp.where(places < fixed, places, moved)]].set(jnp.asarray(sizes, jnp.int32))

    sizes = jnp.where(number % 4 == 0, named(crowded, number // 4), named(usual, number - number // 4 - 1))
    mixed = jax.random.permutation(jax.random.fold_in(own, 3), count)
    source_of, taker = mixed[0:count // 2 * 2:2], mixed[1:count // 2 * 2:2]
    room = jnp.minimum(sizes[source_of] - 1, most - sizes[taker]) // 2
    room = jnp.where((source_of == sequence[0]) | (taker == sequence[0]) | (sizes[taker] == 0), 0, jnp.maximum(room, 0))
    moved = jax.random.randint(jax.random.fold_in(own, 4), (count // 2,), 0, 1 << 20) % (room + 1)
    sizes = sizes.at[source_of].add(-moved).at[taker].add(moved)
    items = jnp.searchsorted(jnp.cumsum(sizes), jnp.arange(rows * top), side="right").astype(jnp.int32)
    listing = items.reshape(top, rows).T
    listing = listing[jax.random.permutation(jax.random.fold_in(own, 1), rows)]
    offset_by = jax.random.randint(jax.random.fold_in(own, 2), (rows, 1), 0, top)
    return jnp.take_along_axis(listing, (jnp.arange(top)[None, :] + offset_by) % top, axis=1)


def load_shares(amount, total, reach, slope, full):
    loads = [(1 << 20) // math.isqrt(grade ** slope) + 1 for grade in range(1, amount + 1)]
    largest = reach if full else min(reach, max(-(-total // amount), total * loads[0] // sum(loads)))
    least = 1 if total - largest >= amount - 1 else 0
    holding, rest = [largest] + [least] * (amount - 1), total - largest - least * (amount - 1)
    while rest > 0:
        movable = [i for i in range(1, amount) if holding[i] < largest] or [i for i in range(1, amount) if holding[i] < reach]
        pool, remaining = sum([loads[i] for i in movable]), rest
        for i in movable:
            addition = min(reach - holding[i], max(1, remaining * loads[i] // pool), rest)
            holding[i] = holding[i] + addition
            rest = rest - addition
    return np.array(holding)


def setup_inputs(seed: int = 0, part: int = 0) -> dict:
    seeds = jax.random.split(jax.random.key(seed), 7)
    part_splits = jax.random.split(jax.random.fold_in(seeds[6], part), 7)
    slowness = jnp.clip(jnp.exp(math.log(1.0) - 1.3862944 * jax.random.uniform(part_splits[0], (NROWS, W), jnp.float32) ** block_levels(part_splits[0], (NROWS, W), ((0, 16),), -0.2, 0.2)), 0.25, 1.0)
    ocean = set_ends((jax.random.randint(part_splits[1], (NROWS, W), 0, 10) < 9).astype(jnp.int32), jax.random.fold_in(part_splits[1], 1), 0, 1)
    start_times = draw_start_times(jax.random.fold_in(jax.random.fold_in(seeds[6], part), 71), part)
    source_cells = set_ends(jax.random.randint(part_splits[3], (SOURCES,), 0, NROWS * W), jax.random.fold_in(part_splits[3], 1), 0, (NROWS * W) - 1).astype(jnp.int32)
    gauge_cells = set_ends(jax.random.randint(part_splits[4], (GAUGES,), 0, R_DEV * W), jax.random.fold_in(part_splits[4], 1), 0, (R_DEV * W) - 1).astype(jnp.int32)
    gauge_owner_keys = jax.random.split(jax.random.fold_in(part_splits[5], 1), GAUGES // G_DEV)
    gauge_owner_turns = jax.random.permutation(jax.random.fold_in(part_splits[5], 3), GAUGES // G_DEV)
    gauge_owner = jax.vmap(lambda own, number: routed_block(jax.random.fold_in(part_splits[5], 2), own, number, G_DEV, N_SPACE, 1, CAP, 2))(gauge_owner_keys, gauge_owner_turns).reshape((GAUGES, 1))
    return {"slowness": slowness, "ocean": ocean, "start_times": start_times, "source_cells": source_cells, "gauge_cells": gauge_cells, "gauge_owner": gauge_owner}


far_value = 1.0e6
land_cost = 1.0e4
clip_value = 48.0
root_two = 1.41421356
root_five = 2.23606798


def relax(padded, cost):
    height = padded.shape[1] - 4
    width = padded.shape[2] - 4

    def shifted(drow, dcol):
        return padded[:, 2 + drow:2 + drow + height, 2 + dcol:2 + dcol + width]

    near = jnp.minimum(jnp.minimum(shifted(0, 1), shifted(0, -1)), jnp.minimum(shifted(1, 0), shifted(-1, 0)))
    diag = jnp.minimum(jnp.minimum(shifted(1, 1), shifted(1, -1)), jnp.minimum(shifted(-1, 1), shifted(-1, -1)))
    knight = jnp.minimum(jnp.minimum(shifted(1, 2), shifted(1, -2)), jnp.minimum(shifted(-1, 2), shifted(-1, -2)))
    knight = jnp.minimum(knight, jnp.minimum(jnp.minimum(shifted(2, 1), shifted(2, -1)), jnp.minimum(shifted(-2, 1), shifted(-2, -1))))
    best = jnp.minimum(near + cost, diag + root_two * cost)
    best = jnp.minimum(best, knight + root_five * cost)
    return jnp.minimum(shifted(0, 0), best)


def reference(slowness, ocean, start_times, source_cells, gauge_cells, gauge_owner):
    cost = jnp.where(ocean == 1, slowness, jnp.float32(land_cost))
    flat = jnp.arange(NROWS * W, dtype=jnp.int32).reshape(NROWS, W)
    seeded = jnp.where(flat[None] == source_cells[:, None, None], jnp.float32(0.0), start_times)

    def sweep(step, field):
        padded = jnp.pad(field, ((0, 0), (2, 2), (2, 2)), constant_values=far_value)
        return relax(padded, cost)

    def settle(field):
        return lax.fori_loop(0, BLOCKS * SWEEPS, sweep, field[None])[0]

    times = lax.map(settle, seeded)
    each_arrival = jnp.minimum(times, jnp.float32(clip_value)) / clip_value
    arrival = jnp.min(each_arrival, axis=0)
    blocks = each_arrival.reshape(SOURCES, N_SPACE, R_DEV * W)
    cells = gauge_cells.reshape(N_SPACE, G_DEV)
    values = jnp.take_along_axis(blocks, cells[None], axis=2)
    owners = gauge_owner.reshape(N_SPACE, G_DEV)
    onehot = (owners[:, :, None] == jnp.arange(N_SPACE, dtype=jnp.int32)[None, None, :]).astype(jnp.int32)
    ranks = jnp.sum((jnp.cumsum(onehot, axis=1) - 1) * onehot, axis=2)
    holder = jnp.arange(N_SPACE, dtype=jnp.int32)[:, None] * CAP + ranks
    result = jnp.zeros((N_SPACE, SOURCES, N_SPACE * CAP), jnp.float32)
    moved = jnp.transpose(values, (1, 2, 0)).reshape(N_SPACE * G_DEV, SOURCES)
    result = result.at[owners.reshape(-1), :, holder.reshape(-1)].set(moved)
    return arrival, result
```

```python
import functools
import jax
import jax.numpy as jnp
from jax import lax
from jax.experimental import pallas as pl
from jax.experimental.pallas import tpu as pltpu
from jax.sharding import PartitionSpec as P

SWEEPS = 8
BLOCKS = 3
ROUNDS = 2

far_value = 1000000.0
land_cost = 10000.0
clip_value = 48.0
root_two = 1.41421356
root_five = 2.23606798

PLANE = 4
LANES = 128
SIDE = 64
PAD = 8
ANY = pl.BlockSpec(memory_space=pl.ANY)
SMEM = pl.BlockSpec(memory_space=pltpu.SMEM)
VMEM = pl.BlockSpec(memory_space=pltpu.VMEM)


def run_copies(copies):
    for copy in copies:
        copy.start()
    for copy in copies:
        copy.wait()


def pack_kernel(groups, cap, place_ref, source_ref, slow_ref, ocean_ref, start_ref, gauge_ref, *rest):
    outs, (cut, sem) = rest[:-2], rest[-2:]
    rows, width = slow_ref.shape
    own = width // PLANE
    tiles = own // LANES
    member = place_ref[0]
    first_row = place_ref[2]
    lane = lax.broadcasted_iota(jnp.int32, (rows, LANES), 1)
    row = lax.broadcasted_iota(jnp.int32, (rows, LANES), 0)
    far = jnp.full((rows, LANES), far_value, jnp.float32)

    def window(field, base):
        for w in range(PLANE):
            for t in range(tiles):
                cut[w, base + t] = field(w * tiles + t)
            right = field((w + 1) * tiles) if w < PLANE - 1 else far
            left = field(w * tiles - 1) if w > 0 else far
            cut[w, base + tiles] = jnp.where(lane < SIDE, right, left)

    def cost(t):
        at = slice(t * LANES, (t + 1) * LANES)
        return jnp.where(ocean_ref[:, at] == 1, slow_ref[:, at], jnp.float32(land_cost))

    def times(s):
        def tile(t):
            flat = (first_row + row) * width + (t * LANES + lane)
            return jnp.where(flat == source_ref[s], 0.0, start_ref[s, :, t * LANES : (t + 1) * LANES])

        return tile

    base = 0
    for number, group in enumerate(groups):
        for s in group:
            window(times(s), base)
            base += tiles + 1
        if number == 0:
            window(cost, base)
            base += tiles + 1
            owner = gauge_ref[2:3, :].astype(jnp.float32)
            across = jnp.broadcast_to(owner, (LANES, LANES))
            down = jnp.transpose(across)
            earlier = lax.broadcasted_iota(jnp.int32, (LANES, LANES), 0) < lax.broadcasted_iota(
                jnp.int32, (LANES, LANES), 1
            )
            same = jnp.where(earlier & (across == down), 1.0, 0.0)
            slot = owner * cap + jnp.sum(same, axis=0, keepdims=True)
            spots = gauge_ref[...].astype(jnp.float32)
            head = lax.broadcasted_iota(jnp.int32, spots.shape, 0)
            meta = jnp.where(head == 2, slot, spots)
            for w in range(PLANE):
                cut[w, base, 0:8] = meta
                cut[w, base, 8:rows] = jnp.zeros((rows - 8, LANES), jnp.float32)
            base += 1
    copies = []
    start = 0
    for number in range(len(groups)):
        for j in range(PLANE):
            out = outs[number * PLANE + j]
            size = out.shape[0]
            copies.append(
                pltpu.make_async_copy(
                    cut.at[member ^ j, start : start + size], out, sem.at[number * PLANE + j]
                )
            )
        start += size
    run_copies(copies)


def edge_kernel(slabs, halo, place_ref, p0, p1, p2, p3, even_ref, odd_ref, full, sem):
    member, plane = place_ref[0], place_ref[1]
    rows = p0.shape[1]
    total = PLANE * rows
    run_copies(
        [
            pltpu.make_async_copy(
                p.at[0:slabs], full.at[:, pl.ds(pl.multiple_of((member ^ j) * rows, 8), rows)], sem.at[j]
            )
            for j, p in enumerate((p0, p1, p2, p3))
        ]
    )
    parity = lax.rem(plane, 2)
    low = pl.multiple_of((1 - parity) * (total - halo), 8)
    high = pl.multiple_of(parity * (total - halo), 8)
    run_copies(
        [
            pltpu.make_async_copy(full.at[:, pl.ds(low, halo)], even_ref, sem.at[0]),
            pltpu.make_async_copy(full.at[:, pl.ds(high, halo)], odd_ref, sem.at[1]),
        ]
    )


def relax_rows(src, dst, cost, count, tiles, start):
    lane = lax.broadcasted_iota(jnp.int32, (8, LANES), 1)
    first, last = lane == 0, lane == LANES - 1

    def from_left(field):
        turned = [pltpu.roll(v, 1, 1) for v in field]
        return [jnp.where(first, turned[t - 1], turned[t]) for t in range(tiles)]

    def from_right(field):
        turned = [pltpu.roll(v, LANES - 1, 1) for v in field]
        return [jnp.where(last, turned[(t + 1) % tiles], turned[t]) for t in range(tiles)]

    c1 = [cost[t, pl.ds(start, 8)] for t in range(tiles)]
    c2 = [root_two * v for v in c1]
    c5 = [root_five * v for v in c1]
    for s in range(count):
        here, one, two = [], [], []
        for t in range(tiles):
            at = s * tiles + t
            here.append(src[at, pl.ds(start, 8)])
            one.append(jnp.minimum(src[at, pl.ds(start - 1, 8)], src[at, pl.ds(start + 1, 8)]))
            two.append(jnp.minimum(src[at, pl.ds(start - 2, 8)], src[at, pl.ds(start + 2, 8)]))
        left, right = from_left(one), from_right(one)
        wide_left = from_left([jnp.minimum(a, b) for a, b in zip(left, two)])
        wide_right = from_right([jnp.minimum(a, b) for a, b in zip(right, two)])
        here_left, here_right = from_left(here), from_right(here)
        for t in range(tiles):
            m1 = jnp.minimum(one[t], jnp.minimum(here_left[t], here_right[t]))
            m2 = jnp.minimum(left[t], right[t])
            m5 = jnp.minimum(wide_left[t], wide_right[t])
            best = jnp.minimum(jnp.minimum(m1 + c1[t], m2 + c2[t]), m5 + c5[t])
            dst[s * tiles + t, pl.ds(start, 8)] = jnp.minimum(here[t], best)


def run_sweeps(first, second, cost, count, tiles, sweeps):
    groups = (first.shape[1] - 2 * PAD) // 8

    def sweep(src, dst, number):
        low = (2 * number) // 8

        def group(at, carry):
            relax_rows(src, dst, cost, count, tiles, pl.multiple_of(PAD + at * 8, 8))
            return carry

        lax.fori_loop(low, groups - low, group, 0)

    def pair(at, carry):
        sweep(first, second, 2 * at + 1)
        sweep(second, first, 2 * at + 2)
        return carry

    lax.fori_loop(0, sweeps // 2, pair, 0)


def halo_copies(plane, halo, total, even, odd, dst, sem, slabs):
    parity = lax.rem(plane, 2)
    above, below = PAD, PAD + halo + total
    even_at = pl.multiple_of(parity * above + (1 - parity) * below, 8)
    odd_at = pl.multiple_of((1 - parity) * above + parity * below, 8)
    copies = [
        pltpu.make_async_copy(even.at[slabs], dst.at[:, pl.ds(even_at, halo)], sem.at[0]),
        pltpu.make_async_copy(odd.at[slabs], dst.at[:, pl.ds(odd_at, halo)], sem.at[1]),
    ]
    return copies, odd_at


def fence(plane, planes, odd_at, halo, field):
    @pl.when((plane == 0) | (plane == planes - 1))
    def _():
        for t in range(field.shape[0]):
            field[t, pl.ds(odd_at, halo)] = jnp.full((halo, LANES), far_value, jnp.float32)


def first_kernel(count, sweeps, has_cost, planes, place_ref, p0, p1, p2, p3, even, odd, *rest):
    if has_cost:
        state, low_ref, high_ref, cost_out, one, two, cost, sem = rest
    else:
        cost_in, state, low_ref, high_ref, one, two, cost, sem = rest
    member, plane = place_ref[0], place_ref[1]
    rows, halo = p0.shape[1], even.shape[1]
    total = PLANE * rows
    tiles = cost.shape[0]
    size = count * tiles
    copies = [
        pltpu.make_async_copy(
            p.at[0:size],
            one.at[:, pl.ds(pl.multiple_of(PAD + halo + (member ^ j) * rows, 8), rows)],
            sem.at[4 + j],
        )
        for j, p in enumerate((p0, p1, p2, p3))
    ]
    halos, odd_at = halo_copies(plane, halo, total, even, odd, one, sem, slice(0, size))
    copies += halos
    if has_cost:
        more, _ = halo_copies(
            plane, halo, total, even, odd, cost, sem.at[pl.ds(2, 2)], slice(size, size + tiles)
        )
        copies += more
        copies += [
            pltpu.make_async_copy(
                p.at[size : size + tiles],
                cost.at[:, pl.ds(pl.multiple_of(PAD + halo + (member ^ j) * rows, 8), rows)],
                sem.at[8 + j],
            )
            for j, p in enumerate((p0, p1, p2, p3))
        ]
    else:
        copies.append(pltpu.make_async_copy(cost_in, cost, sem.at[8]))
    run_copies(copies)
    fence(plane, planes, odd_at, halo, one)
    if has_cost:
        fence(plane, planes, odd_at, halo, cost)
    run_sweeps(one, two, cost, count, tiles, sweeps)
    parity = lax.rem(plane, 2)
    top, bottom = PAD + halo, PAD + halo + total - halo
    low = pl.multiple_of(parity * top + (1 - parity) * bottom, 8)
    high = pl.multiple_of((1 - parity) * top + parity * bottom, 8)
    copies = [
        pltpu.make_async_copy(one.at[:, pl.ds(low, halo)], low_ref, sem.at[0]),
        pltpu.make_async_copy(one.at[:, pl.ds(high, halo)], high_ref, sem.at[1]),
        pltpu.make_async_copy(one.at[:, PAD + halo : PAD + halo + total], state, sem.at[2]),
    ]
    if has_cost:
        copies.append(pltpu.make_async_copy(cost, cost_out, sem.at[3]))
    run_copies(copies)


def last_kernel(count, sweeps, is_last, planes, place_ref, state, even, odd, cost_in, m0, m1, m2, m3, *rest):
    if is_last:
        partial_ref, placed_ref, r0, r1, r2, r3, one, two, cost, meta, best, sem = rest
    else:
        placed_ref, best, one, two, cost, meta, sem = rest
    member, plane = place_ref[0], place_ref[1]
    total, halo = state.shape[1], even.shape[1]
    rows = total // PLANE
    tiles = cost.shape[0]
    own = tiles - 1
    copies = [
        pltpu.make_async_copy(state, one.at[:, PAD + halo : PAD + halo + total], sem.at[2]),
        pltpu.make_async_copy(cost_in, cost, sem.at[3]),
    ]
    copies += [
        pltpu.make_async_copy(m.at[m.shape[0] - 1], meta.at[member ^ j], sem.at[4 + j])
        for j, m in enumerate((m0, m1, m2, m3))
    ]
    halos, odd_at = halo_copies(plane, halo, total, even, odd, one, sem, slice(0, count * tiles))
    run_copies(copies + halos)
    fence(plane, planes, odd_at, halo, one)
    run_sweeps(one, two, cost, count, tiles, sweeps)

    for t in range(own):
        low = None
        for s in range(count):
            at = (s * tiles + t, slice(PAD + halo, PAD + halo + total))
            each = jnp.minimum(one[at], jnp.float32(clip_value)) / clip_value
            one[at] = each
            low = each if low is None else jnp.minimum(low, each)
        best[t] = jnp.minimum(low, partial_ref[t]) if is_last else low
    copies = []
    if is_last:
        copies = [
            pltpu.make_async_copy(
                best.at[:, pl.ds(pl.multiple_of((member ^ j) * rows, 8), rows)], r, sem.at[j]
            )
            for j, r in enumerate((r0, r1, r2, r3))
        ]
        for copy in copies:
            copy.start()

    slots = placed_ref.shape[1]
    lane = lax.broadcasted_iota(jnp.int32, (LANES, LANES), 1).astype(jnp.float32)
    spot = lax.broadcasted_iota(jnp.int32, (LANES, slots), 1).astype(jnp.float32)
    filler = jnp.zeros((LANES - meta.shape[1], LANES), jnp.float32)
    offset = (member * (own * rows)).astype(jnp.float32)
    for q in range(PLANE):
        turned = jnp.transpose(jnp.concatenate([meta[q], filler], axis=0))
        pick = jnp.where(turned[:, 0:1] - offset == lane, 1.0, 0.0).astype(jnp.bfloat16)
        at_lane = turned[:, 1:2] == lane
        at_slot = turned[:, 2:3] == spot
        for s in range(count):
            block = one[s * tiles : s * tiles + own, PAD + halo + q * rows : PAD + halo + (q + 1) * rows]
            rest_of = block.reshape(own * rows, LANES)
            found = jnp.zeros((LANES, LANES), jnp.float32)
            for _ in range(3):
                part = rest_of.astype(jnp.bfloat16)
                rest_of = rest_of - part.astype(jnp.float32)
                found = found + jnp.dot(pick, part, preferred_element_type=jnp.float32)
            value = jnp.sum(jnp.where(at_lane, found, 0.0), axis=1, keepdims=True)
            placed_ref[s * PLANE + q : s * PLANE + q + 1] = jnp.sum(
                jnp.where(at_slot, value, 0.0), axis=0, keepdims=True
            )
    for copy in copies:
        copy.wait()


def join_kernel(place_ref, r0, r1, r2, r3, out_ref):
    member = place_ref[0]
    tiles, rows, _ = r0.shape
    for j, r in enumerate((r0, r1, r2, r3)):
        base = (member ^ j) * (tiles * LANES)
        for t in range(tiles):
            out_ref[:, pl.ds(pl.multiple_of(base + t * LANES, LANES), LANES)] = r[t]


def shape_of(*dims):
    return jax.ShapeDtypeStruct(dims, jnp.float32)


def on_device(slowness, ocean, start_times, source_cells, gauge_cells, gauge_owner):
    axis = "space"
    index = lax.axis_index(axis)
    n = lax.axis_size(axis)
    rows, width = slowness.shape
    sources = start_times.shape[0]
    gauges = gauge_cells.shape[0]
    planes = n // PLANE
    assert n % (2 * PLANE) == 0 and width % (PLANE * LANES) == 0
    assert gauges == LANES and rows * (width // PLANE) == LANES * LANES and sources % 2 == 0
    sweeps = SWEEPS * BLOCKS // ROUNDS
    halo = 2 * sweeps
    total = rows * PLANE
    tiles = width // PLANE // LANES + 1
    assert 2 * SWEEPS * BLOCKS <= SIDE and halo <= total and sweeps % 2 == 0 and halo % 8 == 0
    cap = max(2, 2 * gauges // n)
    half = sources // 2
    groups = (tuple(range(half)), tuple(range(half, sources)))
    plane = index // PLANE
    place = jnp.stack([index % PLANE, plane, index * rows]).astype(jnp.int32)
    column, line = gauge_cells % width, gauge_cells // width
    spots = jnp.stack(
        [(column // LANES) * rows + line, column % LANES, gauge_owner[:, 0]]
        + [jnp.zeros_like(gauge_cells)] * 5
    )

    sizes = [half * tiles + tiles + 1, half * tiles]
    packed = pl.pallas_call(
        functools.partial(pack_kernel, groups, cap),
        out_shape=[shape_of(size, rows, LANES) for size in sizes for _ in range(PLANE)],
        in_specs=[SMEM, SMEM, VMEM, VMEM, VMEM, VMEM],
        out_specs=[ANY] * (2 * PLANE),
        scratch_shapes=[
            pltpu.VMEM((PLANE, sum(sizes), rows, LANES), jnp.float32),
            pltpu.SemaphoreType.DMA((2 * PLANE,)),
        ],
        name="pack",
    )(place, source_cells, slowness, ocean, start_times, spots)

    def swap(x, j):
        return lax.ppermute(x, axis, [(d, d ^ j) for d in range(n)])

    def swap_planes(even, odd):
        pairs_even = [(d, (d // PLANE ^ 1) * PLANE + d % PLANE) for d in range(n)]
        pairs_odd = [
            (d, (((d // PLANE + 1) ^ 1) - 1) * PLANE + d % PLANE)
            for d in range(PLANE, n - PLANE)
        ]
        return lax.ppermute(even, axis, pairs_even), lax.ppermute(odd, axis, pairs_odd)

    pieces = [
        [packed[k * PLANE]] + [swap(packed[k * PLANE + j], j) for j in range(1, PLANE)]
        for k in range(2)
    ]
    halos = []
    for k in range(2):
        slabs = half * tiles + (tiles if k == 0 else 0)
        even, odd = pl.pallas_call(
            functools.partial(edge_kernel, slabs, halo),
            out_shape=[shape_of(slabs, halo, LANES)] * 2,
            in_specs=[SMEM] + [ANY] * 4,
            out_specs=[ANY] * 2,
            scratch_shapes=[
                pltpu.VMEM((slabs, total, LANES), jnp.float32),
                pltpu.SemaphoreType.DMA((PLANE,)),
            ],
            name=f"edge{k}",
        )(place, *pieces[k])
        halos.append(swap_planes(even, odd))

    deep = total + 2 * halo + 2 * PAD
    size = half * tiles
    scratch = [
        pltpu.VMEM((size, deep, LANES), jnp.float32),
        pltpu.VMEM((size, deep, LANES), jnp.float32),
        pltpu.VMEM((tiles, deep, LANES), jnp.float32),
    ]
    states, later = [], []
    cost = None
    for k in range(2):
        outs = pl.pallas_call(
            functools.partial(first_kernel, half, sweeps, k == 0, planes),
            out_shape=[shape_of(size, total, LANES)]
            + [shape_of(size, halo, LANES)] * 2
            + ([shape_of(tiles, deep, LANES)] if k == 0 else []),
            in_specs=[SMEM] + [ANY] * (6 if k == 0 else 7),
            out_specs=[ANY] * (4 if k == 0 else 3),
            scratch_shapes=scratch + [pltpu.SemaphoreType.DMA((12,))],
            name=f"first{k}",
        )(place, *pieces[k], *halos[k], *([] if k == 0 else [cost]))
        if k == 0:
            cost = outs[3]
        states.append(outs[0])
        later.append(swap_planes(outs[1], outs[2]))

    own = tiles - 1
    slots = n * cap
    placed = []
    partial = None
    for k in range(2):
        is_last = k == 1
        out_shape = [shape_of(half * PLANE, slots)]
        out_specs = [VMEM]
        more = [pltpu.VMEM((PLANE, rows, LANES), jnp.float32)]
        if is_last:
            out_shape += [shape_of(own, rows, LANES)] * PLANE
            out_specs += [ANY] * PLANE
            more.append(pltpu.VMEM((own, total, LANES), jnp.float32))
        else:
            out_shape.append(shape_of(own, total, LANES))
            out_specs.append(VMEM)
        outs = pl.pallas_call(
            functools.partial(last_kernel, half, sweeps, is_last, planes),
            out_shape=out_shape,
            in_specs=[SMEM] + [ANY] * 8 + ([VMEM] if is_last else []),
            out_specs=out_specs,
            scratch_shapes=scratch + more + [pltpu.SemaphoreType.DMA((8,))],
            name=f"last{k}",
        )(place, states[k], *later[k], cost, *pieces[0], *([partial] if is_last else []))
        placed.append(outs[0])
        if is_last:
            returned = outs[1:]
        else:
            partial = outs[1]

    arrival = pl.pallas_call(
        join_kernel,
        out_shape=shape_of(rows, width),
        in_specs=[SMEM] + [VMEM] * PLANE,
        out_specs=VMEM,
        name="join",
    )(place, returned[0], *[swap(returned[j], j) for j in range(1, PLANE)])

    sent = jnp.concatenate(placed, axis=0).reshape(sources * PLANE, n, cap).transpose(1, 0, 2)
    received = lax.all_to_all(sent, axis, split_axis=0, concat_axis=0, tiled=True)
    joined = jnp.sum(received.reshape(planes, PLANE, sources, PLANE, cap), axis=1)
    result = joined.transpose(1, 0, 2, 3).reshape(1, sources, n * cap)
    return (arrival, result)


def solution(mesh):
    return jax.shard_map(
        on_device,
        mesh=mesh,
        in_specs=(
            P(("groups", "space"), None),
            P(("groups", "space"), None),
            P("groups", "space", None),
            P("groups"),
            P(("groups", "space")),
            P(("groups", "space"), None),
        ),
        out_specs=(P(("groups", "space"), None), P(("groups", "space"), None, None)),
        check_vma=False,
    )
```

```python
import functools
import jax
import jax.numpy as jnp
from jax import lax
from jax.experimental import pallas as pl
from jax.experimental.pallas import tpu as pltpu
from jax.sharding import PartitionSpec as P

SWEEPS = 8
BLOCKS = 3
ROUNDS = 2

far_value = 1000000.0
land_cost = 10000.0
clip_value = 48.0
root_two = 1.41421356
root_five = 2.23606798

PLANE = 4
LANES = 128
SIDE = 64
PAD = 8
VMEM_BYTES = 24 * 1024 * 1024
ANY = pl.BlockSpec(memory_space=pl.ANY)
SMEM = pl.BlockSpec(memory_space=pltpu.SMEM)
VMEM = pl.BlockSpec(memory_space=pltpu.VMEM)


def run_copies(copies):
    for copy in copies:
        copy.start()
    for copy in copies:
        copy.wait()


def inverse(number):
    return pow(number, -1, LANES)


def spread(tiles):
    shape = (8, LANES)
    lane = lax.broadcasted_iota(jnp.int32, shape, 1)
    for j in range(tiles):
        chunk = ((lane + (LANES - j)) * inverse(tiles)) & (LANES - 1)
        tile_of = (chunk * tiles + j) >> 7
        masks = [tile_of == t for t in range(1, tiles)]
        order = (lane * tiles + j) & (LANES - 1)
        yield j, masks, order


def gather_lanes(x, order):
    return jnp.take_along_axis(x, order, axis=1, mode="promise_in_bounds")


def here():
    index = lax.axis_index("space")
    return lax.rem(index, PLANE), lax.div(index, PLANE), index


def pack_kernel(groups, cap, source_ref, slow_ref, ocean_ref, start_ref, cell_ref, owner_ref, *rest):
    outs, (plain, cut, sem) = rest[:-3], rest[-3:]
    rows, width = slow_ref.shape
    own = width // PLANE
    tiles = own // LANES
    chunk = tiles + 1
    member, _, index = here()
    first_row = index * rows
    lane = lax.broadcasted_iota(jnp.int32, (rows, LANES), 1)
    row = lax.broadcasted_iota(jnp.int32, (rows, LANES), 0)
    far = jnp.full((rows, LANES), far_value, jnp.float32)

    def window(field, at):
        for w in range(PLANE):
            for t in range(tiles):
                plain[w, at, t] = field(w * tiles + t)
            right = field((w + 1) * tiles) if w < PLANE - 1 else far
            left = field(w * tiles - 1) if w > 0 else far
            plain[w, at, tiles] = jnp.where(lane < SIDE, right, left)

    def cost(t):
        at = slice(t * LANES, (t + 1) * LANES)
        return jnp.where(ocean_ref[:, at] == 1, slow_ref[:, at], jnp.float32(land_cost))

    def times(s):
        def tile(t):
            flat = (first_row + row) * width + (t * LANES + lane)
            return jnp.where(flat == source_ref[s], 0.0, start_ref[s, :, t * LANES : (t + 1) * LANES])

        return tile

    fields = []
    for number, group in enumerate(groups):
        fields += [times(s) for s in group]
        if number == 0:
            fields.append(cost)
    for at, field in enumerate(fields):
        window(field, at)
    bases, base = [], 0
    for number, group in enumerate(groups):
        for _ in range(len(group) + (number == 0)):
            bases.append(base)
            base += chunk
        if number == 0:
            meta_at = base
            base += 1

    for j, masks, order in spread(chunk):
        for at in range(len(fields)):
            def convert(w, carry, at=at):
                for half in range(0, rows, 8):
                    mixed = plain[w, at, 0, half : half + 8]
                    for t, mask in enumerate(masks):
                        mixed = jnp.where(mask, plain[w, at, t + 1, half : half + 8], mixed)
                    cut[w, bases[at] + j, half : half + 8] = gather_lanes(mixed, order)
                return carry

            lax.fori_loop(0, PLANE, convert, 0)

    owner = owner_ref[...].astype(jnp.float32)
    across = jnp.broadcast_to(owner, (LANES, LANES))
    down = jnp.transpose(across)
    earlier = lax.broadcasted_iota(jnp.int32, (LANES, LANES), 0) < lax.broadcasted_iota(
        jnp.int32, (LANES, LANES), 1
    )
    rank = jnp.sum(jnp.where(earlier & (across == down), 1.0, 0.0), axis=0, keepdims=True)
    cell = cell_ref[...].astype(jnp.float32)
    line = jnp.floor(cell / width)
    column = cell - line * width
    part = jnp.floor(column / own)
    column = column - part * own
    spot = jnp.floor((column + 0.5) / chunk)
    place = (part * chunk + (column - spot * chunk)) * rows + line
    filler = jnp.zeros((rows - 4, LANES), jnp.float32)
    meta = jnp.concatenate([place, spot, owner, rank, filler], axis=0)
    for w in range(PLANE):
        cut[w, meta_at] = meta

    copies = []
    start = 0
    for number in range(len(groups)):
        for j in range(PLANE):
            out = outs[number * PLANE + j]
            size = out.shape[0]
            copies.append(
                pltpu.make_async_copy(
                    cut.at[member ^ j, start : start + size], out, sem.at[number * PLANE + j]
                )
            )
        start += size
    run_copies(copies)


def edge_kernel(slabs, halo, p0, p1, p2, p3, even_ref, odd_ref, full, sem):
    member, plane, _ = here()
    rows = p0.shape[1]
    total = PLANE * rows
    run_copies(
        [
            pltpu.make_async_copy(
                p.at[0:slabs], full.at[:, pl.ds(pl.multiple_of((member ^ j) * rows, 8), rows)], sem.at[j]
            )
            for j, p in enumerate((p0, p1, p2, p3))
        ]
    )
    parity = lax.rem(plane, 2)
    low = pl.multiple_of((1 - parity) * (total - halo), 8)
    high = pl.multiple_of(parity * (total - halo), 8)
    run_copies(
        [
            pltpu.make_async_copy(full.at[:, pl.ds(low, halo)], even_ref, sem.at[0]),
            pltpu.make_async_copy(full.at[:, pl.ds(high, halo)], odd_ref, sem.at[1]),
        ]
    )


def relax_rows(src, dst, cost, count, tiles, start):
    def ends(field, reach):
        before = [pltpu.roll(field[tiles - k], 1, 1) for k in range(reach, 0, -1)]
        after = [pltpu.roll(field[k], LANES - 1, 1) for k in range(reach)]
        return before + field + after

    for s in range(count):
        near, one, two = [], [], []
        for t in range(tiles):
            at = s * tiles + t
            near.append(src[at, pl.ds(start, 8)])
            one.append(jnp.minimum(src[at, pl.ds(start - 1, 8)], src[at, pl.ds(start + 1, 8)]))
            two.append(jnp.minimum(src[at, pl.ds(start - 2, 8)], src[at, pl.ds(start + 2, 8)]))
        near, one, two = ends(near, 1), ends(one, 2), ends(two, 1)
        for t in range(tiles):
            m1 = jnp.minimum(one[t + 2], jnp.minimum(near[t], near[t + 2]))
            m2 = jnp.minimum(one[t + 1], one[t + 3])
            m5 = jnp.minimum(jnp.minimum(one[t], one[t + 4]), jnp.minimum(two[t], two[t + 2]))
            best = jnp.minimum(m1 + cost[0, t, pl.ds(start, 8)], m2 + cost[1, t, pl.ds(start, 8)])
            best = jnp.minimum(best, m5 + cost[2, t, pl.ds(start, 8)])
            dst[s * tiles + t, pl.ds(start, 8)] = jnp.minimum(near[t + 1], best)


def scale_cost(cost):
    def group(at, carry):
        spot = pl.ds(pl.multiple_of(at * 8, 8), 8)
        for t in range(cost.shape[1]):
            value = cost[0, t, spot]
            cost[1, t, spot] = root_two * value
            cost[2, t, spot] = root_five * value
        return carry

    lax.fori_loop(0, cost.shape[2] // 8, group, 0)


def run_sweeps(first, second, cost, count, tiles, sweeps):
    groups = (first.shape[1] - 2 * PAD) // 8

    def sweep(src, dst, number):
        low = (2 * number) // 8

        def group(at, carry):
            relax_rows(src, dst, cost, count, tiles, pl.multiple_of(PAD + at * 8, 8))
            return carry

        lax.fori_loop(low, groups - low, group, 0)

    def pair(at, carry):
        sweep(first, second, 2 * at + 1)
        sweep(second, first, 2 * at + 2)
        return carry

    lax.fori_loop(0, sweeps // 2, pair, 0)


def halo_copies(plane, halo, total, even, odd, dst, sem, slabs):
    parity = lax.rem(plane, 2)
    above, below = PAD, PAD + halo + total
    even_at = pl.multiple_of(parity * above + (1 - parity) * below, 8)
    odd_at = pl.multiple_of((1 - parity) * above + parity * below, 8)
    copies = [
        pltpu.make_async_copy(even.at[slabs], dst.at[:, pl.ds(even_at, halo)], sem.at[0]),
        pltpu.make_async_copy(odd.at[slabs], dst.at[:, pl.ds(odd_at, halo)], sem.at[1]),
    ]
    return copies, odd_at


def fence(plane, planes, odd_at, halo, field):
    @pl.when((plane == 0) | (plane == planes - 1))
    def _():
        for t in range(field.shape[0]):
            field[t, pl.ds(odd_at, halo)] = jnp.full((halo, LANES), far_value, jnp.float32)


def first_kernel(count, sweeps, has_cost, planes, p0, p1, p2, p3, even, odd, *rest):
    if has_cost:
        state, low_ref, high_ref, cost_out, one, two, cost, sem = rest
    else:
        cost_in, state, low_ref, high_ref, one, two, cost, sem = rest
    member, plane, _ = here()
    rows, halo = p0.shape[1], even.shape[1]
    total = PLANE * rows
    tiles = cost.shape[1]
    size = count * tiles
    base = cost.at[0]
    copies = [
        pltpu.make_async_copy(
            p.at[0:size],
            one.at[:, pl.ds(pl.multiple_of(PAD + halo + (member ^ j) * rows, 8), rows)],
            sem.at[4 + j],
        )
        for j, p in enumerate((p0, p1, p2, p3))
    ]
    halos, odd_at = halo_copies(plane, halo, total, even, odd, one, sem, slice(0, size))
    copies += halos
    if has_cost:
        more, _ = halo_copies(
            plane, halo, total, even, odd, base, sem.at[pl.ds(2, 2)], slice(size, size + tiles)
        )
        copies += more
        copies += [
            pltpu.make_async_copy(
                p.at[size : size + tiles],
                base.at[:, pl.ds(pl.multiple_of(PAD + halo + (member ^ j) * rows, 8), rows)],
                sem.at[8 + j],
            )
            for j, p in enumerate((p0, p1, p2, p3))
        ]
    else:
        copies.append(pltpu.make_async_copy(cost_in, cost, sem.at[8]))
    run_copies(copies)
    fence(plane, planes, odd_at, halo, one)
    if has_cost:
        fence(plane, planes, odd_at, halo, base)
        scale_cost(cost)
    run_sweeps(one, two, cost, count, tiles, sweeps)
    parity = lax.rem(plane, 2)
    top, bottom = PAD + halo, PAD + halo + total - halo
    low = pl.multiple_of(parity * top + (1 - parity) * bottom, 8)
    high = pl.multiple_of((1 - parity) * top + parity * bottom, 8)
    copies = [
        pltpu.make_async_copy(one.at[:, pl.ds(low, halo)], low_ref, sem.at[0]),
        pltpu.make_async_copy(one.at[:, pl.ds(high, halo)], high_ref, sem.at[1]),
        pltpu.make_async_copy(one.at[:, PAD + halo : PAD + halo + total], state, sem.at[2]),
    ]
    if has_cost:
        copies.append(pltpu.make_async_copy(cost, cost_out, sem.at[3]))
    run_copies(copies)


def last_kernel(count, sweeps, is_last, planes, cap, state, even, odd, cost_in, m0, m1, m2, m3, *rest):
    if is_last:
        partial_ref, earlier_ref, placed_ref, r0, r1, r2, r3, one, two, cost, meta, best, plain, sem = rest
    else:
        placed_ref, best, one, two, cost, meta, sem = rest
    member, plane, _ = here()
    total, halo = state.shape[1], even.shape[1]
    rows = total // PLANE
    tiles = cost.shape[1]
    own = tiles - 1
    copies = [
        pltpu.make_async_copy(state, one.at[:, PAD + halo : PAD + halo + total], sem.at[2]),
        pltpu.make_async_copy(cost_in, cost, sem.at[3]),
    ]
    copies += [
        pltpu.make_async_copy(m.at[m.shape[0] - 1], meta.at[member ^ j], sem.at[4 + j])
        for j, m in enumerate((m0, m1, m2, m3))
    ]
    halos, odd_at = halo_copies(plane, halo, total, even, odd, one, sem, slice(0, count * tiles))
    run_copies(copies + halos)
    fence(plane, planes, odd_at, halo, one)
    run_sweeps(one, two, cost, count, tiles, sweeps)

    for t in range(tiles):
        low = None
        for s in range(count):
            at = (s * tiles + t, slice(PAD + halo, PAD + halo + total))
            each = jnp.minimum(one[at], jnp.float32(clip_value)) / clip_value
            one[at] = each
            low = each if low is None else jnp.minimum(low, each)
        best[t] = jnp.minimum(low, partial_ref[t]) if is_last else low
    copies = []
    if is_last:
        lane = lax.broadcasted_iota(jnp.int32, (8, LANES), 1)
        orders = [((lane + (LANES - j)) * inverse(tiles)) & (LANES - 1) for j in range(tiles)]
        chosen = [lax.rem(lane + t * LANES, tiles) for t in range(own)]

        def back(at, carry):
            spot = pl.ds(pl.multiple_of(at * 8, 8), 8)
            turned = [gather_lanes(best[j, spot], orders[j]) for j in range(tiles)]
            for t in range(own):
                value = turned[0]
                for j in range(1, tiles):
                    value = jnp.where(chosen[t] == j, turned[j], value)
                plain[t, spot] = value
            return carry

        lax.fori_loop(0, total // 8, back, 0)
        copies = [
            pltpu.make_async_copy(
                plain.at[:, pl.ds(pl.multiple_of((member ^ j) * rows, 8), rows)], r, sem.at[j]
            )
            for j, r in enumerate((r0, r1, r2, r3))
        ]
        for copy in copies:
            copy.start()

    def exact(pick, value):
        found = None
        for _ in range(3):
            part = value.astype(jnp.bfloat16)
            value = value - part.astype(jnp.float32)
            term = jnp.dot(pick, part, preferred_element_type=jnp.float32)
            found = term if found is None else found + term
        return found

    n, _, slots = placed_ref.shape
    height = tiles * rows
    lane = lax.broadcasted_iota(jnp.int32, (LANES, LANES), 1).astype(jnp.float32)
    place = lax.broadcasted_iota(jnp.int32, (LANES, height), 1).astype(jnp.float32)
    spot = lax.broadcasted_iota(jnp.int32, (LANES, slots), 1).astype(jnp.float32)
    device = lax.broadcasted_iota(jnp.int32, (n, LANES), 0).astype(jnp.float32)
    filler = jnp.zeros((LANES - meta.shape[1], LANES), jnp.float32)
    offset = (member * height).astype(jnp.float32)
    totals = [None] * count
    for q in range(PLANE):
        turned = jnp.transpose(jnp.concatenate([meta[q], filler], axis=0))
        pick = jnp.where(turned[:, 0:1] - offset == place, 1.0, 0.0).astype(jnp.bfloat16)
        at_lane = turned[:, 1:2] == lane
        base = ((plane * PLANE + q) * cap).astype(jnp.float32)
        at_slot = turned[:, 3:4] + base == spot
        to_owner = jnp.where(meta[q, 2:3] == device, 1.0, 0.0).astype(jnp.bfloat16)
        for s in range(count):
            block = one[s * tiles : (s + 1) * tiles, PAD + halo + q * rows : PAD + halo + (q + 1) * rows]
            found = exact(pick, block.reshape(height, LANES))
            value = jnp.sum(jnp.where(at_lane, found, 0.0), axis=1, keepdims=True)
            term = exact(to_owner, jnp.where(at_slot, value, 0.0))
            totals[s] = term if totals[s] is None else totals[s] + term
    if is_last:
        placed_ref[:, 0:count] = earlier_ref[...]
        for s in range(count):
            placed_ref[:, count + s] = totals[s]
    else:
        for s in range(count):
            placed_ref[:, s] = totals[s]
    for copy in copies:
        copy.wait()


def join_kernel(r0, r1, r2, r3, gauge_ref, out_ref, result_ref):
    member, _, _ = here()
    tiles, rows, _ = r0.shape
    for j, r in enumerate((r0, r1, r2, r3)):
        base = (member ^ j) * (tiles * LANES)
        for t in range(tiles):
            out_ref[:, pl.ds(pl.multiple_of(base + t * LANES, LANES), LANES)] = r[t]
    result_ref[0] = jnp.sum(gauge_ref[...], axis=0)


def shape_of(*dims):
    return jax.ShapeDtypeStruct(dims, jnp.float32)


def on_device(slowness, ocean, start_times, source_cells, gauge_cells, gauge_owner):
    axis = "space"
    index = lax.axis_index(axis)
    n = lax.axis_size(axis)
    rows, width = slowness.shape
    sources = start_times.shape[0]
    gauges = gauge_cells.shape[0]
    planes = n // PLANE
    assert n % (2 * PLANE) == 0 and width % (PLANE * LANES) == 0
    assert gauges == LANES and rows * (width // PLANE) == LANES * LANES and sources % 2 == 0
    sweeps = SWEEPS * BLOCKS // ROUNDS
    halo = 2 * sweeps
    total = rows * PLANE
    tiles = width // PLANE // LANES + 1
    assert 2 * SWEEPS * BLOCKS <= SIDE and halo <= total and sweeps % 2 == 0 and halo % 8 == 0
    cap = max(2, 2 * gauges // n)
    half = sources // 2
    groups = (tuple(range(half)), tuple(range(half, sources)))
    limit = pltpu.CompilerParams(vmem_limit_bytes=VMEM_BYTES)

    sizes = [half * tiles + tiles + 1, half * tiles]
    packed = pl.pallas_call(
        functools.partial(pack_kernel, groups, cap),
        out_shape=[shape_of(size, rows, LANES) for size in sizes for _ in range(PLANE)],
        in_specs=[SMEM, VMEM, VMEM, VMEM, VMEM, VMEM],
        out_specs=[ANY] * (2 * PLANE),
        scratch_shapes=[
            pltpu.VMEM((PLANE, sources + 1, tiles, rows, LANES), jnp.float32),
            pltpu.VMEM((PLANE, sum(sizes), rows, LANES), jnp.float32),
            pltpu.SemaphoreType.DMA((2 * PLANE,)),
        ],
        name="pack",
        compiler_params=limit,
    )(
        source_cells,
        slowness,
        ocean,
        start_times,
        gauge_cells.reshape(1, gauges),
        gauge_owner.reshape(1, gauges),
    )

    def swap(x, j):
        return lax.ppermute(x, axis, [(d, d ^ j) for d in range(n)])

    def swap_planes(even, odd):
        pairs_even = [(d, (d // PLANE ^ 1) * PLANE + d % PLANE) for d in range(n)]
        pairs_odd = [
            (d, (((d // PLANE + 1) ^ 1) - 1) * PLANE + d % PLANE)
            for d in range(PLANE, n - PLANE)
        ]
        return lax.ppermute(even, axis, pairs_even), lax.ppermute(odd, axis, pairs_odd)

    pieces = [
        [packed[k * PLANE]] + [swap(packed[k * PLANE + j], j) for j in range(1, PLANE)]
        for k in range(2)
    ]
    halos = []
    for k in range(2):
        slabs = half * tiles + (tiles if k == 0 else 0)
        even, odd = pl.pallas_call(
            functools.partial(edge_kernel, slabs, halo),
            out_shape=[shape_of(slabs, halo, LANES)] * 2,
            in_specs=[ANY] * 4,
            out_specs=[ANY] * 2,
            compiler_params=limit,
            scratch_shapes=[
                pltpu.VMEM((slabs, total, LANES), jnp.float32),
                pltpu.SemaphoreType.DMA((PLANE,)),
            ],
            name=f"edge{k}",
        )(*pieces[k])
        halos.append(swap_planes(even, odd))

    deep = total + 2 * halo + 2 * PAD
    size = half * tiles
    scratch = [
        pltpu.VMEM((size, deep, LANES), jnp.float32),
        pltpu.VMEM((size, deep, LANES), jnp.float32),
        pltpu.VMEM((3, tiles, deep, LANES), jnp.float32),
    ]
    states, later = [], []
    cost = None
    for k in range(2):
        outs = pl.pallas_call(
            functools.partial(first_kernel, half, sweeps, k == 0, planes),
            out_shape=[shape_of(size, total, LANES)]
            + [shape_of(size, halo, LANES)] * 2
            + ([shape_of(3, tiles, deep, LANES)] if k == 0 else []),
            in_specs=[ANY] * (6 if k == 0 else 7),
            compiler_params=limit,
            out_specs=[ANY] * (4 if k == 0 else 3),
            scratch_shapes=scratch + [pltpu.SemaphoreType.DMA((12,))],
            name=f"first{k}",
        )(*pieces[k], *halos[k], *([] if k == 0 else [cost]))
        if k == 0:
            cost = outs[3]
        states.append(outs[0])
        later.append(swap_planes(outs[1], outs[2]))

    slots = n * cap
    partial, placed = None, None
    for k in range(2):
        is_last = k == 1
        out_shape = [shape_of(n, half * (k + 1), slots)]
        out_specs = [VMEM]
        more = [pltpu.VMEM((PLANE, rows, LANES), jnp.float32)]
        if is_last:
            out_shape += [shape_of(tiles - 1, rows, LANES)] * PLANE
            out_specs += [ANY] * PLANE
            more.append(pltpu.VMEM((tiles, total, LANES), jnp.float32))
            more.append(pltpu.VMEM((tiles - 1, total, LANES), jnp.float32))
        else:
            out_shape.append(shape_of(tiles, total, LANES))
            out_specs.append(VMEM)
        outs = pl.pallas_call(
            functools.partial(last_kernel, half, sweeps, is_last, planes, cap),
            out_shape=out_shape,
            in_specs=[ANY] * 8 + ([VMEM, VMEM] if is_last else []),
            out_specs=out_specs,
            scratch_shapes=scratch + more + [pltpu.SemaphoreType.DMA((8,))],
            compiler_params=limit,
            name=f"last{k}",
        )(states[k], *later[k], cost, *pieces[0], *([partial, placed] if is_last else []))
        placed = outs[0]
        if is_last:
            returned = outs[1:]
        else:
            partial = outs[1]

    back = [returned[0]] + [swap(returned[j], j) for j in range(1, PLANE)]
    received = lax.all_to_all(placed, axis, split_axis=0, concat_axis=0, tiled=True)
    return pl.pallas_call(
        join_kernel,
        out_shape=(shape_of(rows, width), shape_of(1, sources, slots)),
        in_specs=[VMEM] * (PLANE + 1),
        out_specs=(VMEM, VMEM),
        compiler_params=limit,
        name="join",
    )(*back, received)


def solution(mesh):
    return jax.shard_map(
        on_device,
        mesh=mesh,
        in_specs=(
            P(("groups", "space"), None),
            P(("groups", "space"), None),
            P("groups", "space", None),
            P("groups"),
            P(("groups", "space")),
            P(("groups", "space"), None),
        ),
        out_specs=(P(("groups", "space"), None), P(("groups", "space"), None, None)),
        check_vma=False,
    )
```

```python
import functools
import jax
import jax.numpy as jnp
from jax import lax
from jax.experimental import pallas as pl
from jax.experimental.pallas import tpu as pltpu
from jax.sharding import PartitionSpec as P

SWEEPS = 8
BLOCKS = 3
ROUNDS = 2

far_value = 1000000.0
land_cost = 10000.0
clip_value = 48.0
root_two = 1.41421356
root_five = 2.23606798

PLANE = 4
LANES = 128
SIDE = 64
PAD = 8
REACH = 2
VMEM_BYTES = 24 * 1024 * 1024
ANY = pl.BlockSpec(memory_space=pl.ANY)
SMEM = pl.BlockSpec(memory_space=pltpu.SMEM)
VMEM = pl.BlockSpec(memory_space=pltpu.VMEM)


def run_copies(copies):
    for copy in copies:
        copy.start()
    for copy in copies:
        copy.wait()


def inverse(number):
    return pow(number, -1, LANES)


def gather_lanes(x, order):
    return jnp.take_along_axis(x, order, axis=1, mode="promise_in_bounds")


def here():
    index = lax.axis_index("space")
    return lax.rem(index, PLANE), lax.div(index, PLANE), index


def pack_kernel(groups, cap, source_ref, slow_ref, ocean_ref, start_ref, cell_ref, owner_ref, *rest):
    outs, (plain, cut, sem) = rest[:-3], rest[-3:]
    rows, width = slow_ref.shape
    own = width // PLANE
    tiles = own // LANES
    chunk = tiles + 1
    member, _, index = here()
    first_row = index * rows
    lane = lax.broadcasted_iota(jnp.int32, (rows, LANES), 1)
    row = lax.broadcasted_iota(jnp.int32, (rows, LANES), 0)
    far = jnp.full((rows, LANES), far_value, jnp.float32)

    def window(field, at):
        for w in range(PLANE):
            for t in range(tiles):
                plain[w, at, t, 0:rows] = field(w * tiles + t)
            right = field((w + 1) * tiles) if w < PLANE - 1 else far
            left = field(w * tiles - 1) if w > 0 else far
            plain[w, at, tiles, 0:rows] = jnp.where(lane < SIDE, right, left)

    def cost(t):
        at = slice(t * LANES, (t + 1) * LANES)
        return jnp.where(ocean_ref[:, at] == 1, slow_ref[:, at], jnp.float32(land_cost))

    def times(s):
        def tile(t):
            flat = (first_row + row) * width + (t * LANES + lane)
            return jnp.where(flat == source_ref[s], 0.0, start_ref[s, :, t * LANES : (t + 1) * LANES])

        return tile

    fields = []
    for number, group in enumerate(groups):
        fields += [times(s) for s in group]
        if number == 0:
            fields.append(cost)
    for at, field in enumerate(fields):
        window(field, at)
    bases, base = [], 0
    for number, group in enumerate(groups):
        for _ in range(len(group) + (number == 0)):
            bases.append(base)
            base += chunk
        if number == 0:
            meta_at = base
            base += 1

    lane = lax.broadcasted_iota(jnp.int32, (8, LANES), 1)

    def convert(j, carry):
        column = (((lane + (LANES - j)) * inverse(chunk)) & (LANES - 1)) * chunk + j
        masks = [column >= t * LANES for t in range(1, chunk)]
        order = (lane * chunk + j) & (LANES - 1)
        for at in range(len(fields)):
            for w in range(PLANE):
                for half in range(0, rows, 8):
                    mixed = plain[w, at, 0, half : half + 8]
                    for t, mask in enumerate(masks):
                        mixed = jnp.where(mask, plain[w, at, t + 1, half : half + 8], mixed)
                    cut[w, bases[at] + j, half : half + 8] = gather_lanes(mixed, order)
        return carry

    lax.fori_loop(0, chunk, convert, 0)

    owner = owner_ref[...].astype(jnp.float32)
    across = jnp.broadcast_to(owner, (LANES, LANES))
    down = jnp.transpose(across)
    earlier = lax.broadcasted_iota(jnp.int32, (LANES, LANES), 0) < lax.broadcasted_iota(
        jnp.int32, (LANES, LANES), 1
    )
    rank = jnp.sum(jnp.where(earlier & (across == down), 1.0, 0.0), axis=0, keepdims=True)
    cell = cell_ref[...].astype(jnp.float32)
    line = jnp.floor(cell / width)
    column = cell - line * width
    part = jnp.floor(column / own)
    column = column - part * own
    spot = jnp.floor((column + 0.5) / chunk)
    place = (part * chunk + (column - spot * chunk)) * rows + line
    filler = jnp.zeros((rows - 4, LANES), jnp.float32)
    meta = jnp.concatenate([place, spot, owner, rank, filler], axis=0)
    for w in range(PLANE):
        cut[w, meta_at] = meta

    copies = []
    start = 0
    for number in range(len(groups)):
        for j in range(PLANE):
            out = outs[number * PLANE + j]
            size = out.shape[0]
            copies.append(
                pltpu.make_async_copy(
                    cut.at[member ^ j, start : start + size], out, sem.at[number * PLANE + j]
                )
            )
        start += size
    run_copies(copies)


def edge_kernel(slabs, halo, p0, p1, p2, p3, even_ref, odd_ref, full, sem):
    member, plane, _ = here()
    rows = p0.shape[1]
    total = PLANE * rows
    run_copies(
        [
            pltpu.make_async_copy(
                p.at[0:slabs], full.at[:, pl.ds(pl.multiple_of((member ^ j) * rows, 8), rows)], sem.at[j]
            )
            for j, p in enumerate((p0, p1, p2, p3))
        ]
    )
    parity = lax.rem(plane, 2)
    low = pl.multiple_of((1 - parity) * (total - halo), 8)
    high = pl.multiple_of(parity * (total - halo), 8)
    run_copies(
        [
            pltpu.make_async_copy(full.at[:, pl.ds(low, halo)], even_ref, sem.at[0]),
            pltpu.make_async_copy(full.at[:, pl.ds(high, halo)], odd_ref, sem.at[1]),
        ]
    )


def keep_ends(dst, s, t, spot, value, tiles):
    if t < REACH:
        dst[s, tiles + REACH + t, spot] = pltpu.roll(value, LANES - 1, 1)
    if t >= tiles - REACH:
        dst[s, t - (tiles - REACH), spot] = pltpu.roll(value, 1, 1)


def relax_rows(src, dst, cost, count, tiles, start):
    spot = pl.ds(start, 8)
    order = sorted(range(tiles), key=lambda t: REACH <= t < tiles - REACH)
    for s in range(count):

        def load(t, shift):
            return src[s, t + REACH, pl.ds(start + shift, 8)]

        near = {t: load(t, 0) for t in range(-1, tiles + 1)}
        one = {t: jnp.minimum(load(t, -1), load(t, 1)) for t in range(-2, tiles + 2)}
        two = {t: jnp.minimum(load(t, -2), load(t, 2)) for t in range(-1, tiles + 1)}
        for t in order:
            m1 = jnp.minimum(one[t], jnp.minimum(near[t - 1], near[t + 1]))
            m2 = jnp.minimum(one[t - 1], one[t + 1])
            m5 = jnp.minimum(
                jnp.minimum(one[t - 2], one[t + 2]), jnp.minimum(two[t - 1], two[t + 1])
            )
            best = jnp.minimum(m1 + cost[0, t, spot], m2 + cost[1, t, spot])
            best = jnp.minimum(best, m5 + cost[2, t, spot])
            value = jnp.minimum(near[t], best)
            dst[s, t + REACH, spot] = value


def fill_rows(field, tiles, start):
    spot = pl.ds(start, 8)
    for s in range(field.shape[0]):
        for t in list(range(REACH)) + list(range(tiles - REACH, tiles)):
            keep_ends(field, s, t, spot, field[s, t + REACH, spot], tiles)


def fill_ends(field, tiles):
    def group(at, carry):
        for k in range(2):
            fill_rows(field, tiles, pl.multiple_of(PAD + at * 16 + k * 8, 8))
        return carry

    lax.fori_loop(0, (field.shape[2] - 3 * PAD) // 16, group, 0)


def scale_cost(cost):
    def group(at, carry):
        spot = pl.ds(pl.multiple_of(at * 8, 8), 8)
        for t in range(cost.shape[1]):
            value = cost[0, t, spot]
            cost[1, t, spot] = root_two * value
            cost[2, t, spot] = root_five * value
        return carry

    lax.fori_loop(0, cost.shape[2] // 8, group, 0)


def run_sweeps(first, second, cost, count, tiles, sweeps):
    groups = (first.shape[2] - 3 * PAD) // 8

    def sweep(src, dst, number):
        low = (2 * number) // 8

        def group(at, carry):
            start = pl.multiple_of(PAD + (low + 2 * at) * 8, 8)
            fill_rows(dst, tiles, pl.multiple_of(start - 8, 8))
            relax_rows(src, dst, cost, count, tiles, start)
            fill_rows(dst, tiles, start)
            relax_rows(src, dst, cost, count, tiles, pl.multiple_of(start + 8, 8))
            return carry

        lax.fori_loop(0, groups // 2 - low, group, 0)
        fill_rows(dst, tiles, pl.multiple_of(PAD + (groups - low - 1) * 8, 8))

    def pair(at, carry):
        sweep(first, second, 2 * at + 1)
        sweep(second, first, 2 * at + 2)
        return carry

    fill_ends(first, tiles)
    lax.fori_loop(0, sweeps // 2, pair, 0)


def core(field, s, tiles):
    return field.at[s, REACH : REACH + tiles]


def halo_copies(plane, halo, total, even, odd, dst, sem, slabs):
    parity = lax.rem(plane, 2)
    above, below = PAD, PAD + halo + total
    even_at = pl.multiple_of(parity * above + (1 - parity) * below, 8)
    odd_at = pl.multiple_of((1 - parity) * above + parity * below, 8)
    copies = [
        pltpu.make_async_copy(even.at[slabs], dst.at[:, pl.ds(even_at, halo)], sem.at[0]),
        pltpu.make_async_copy(odd.at[slabs], dst.at[:, pl.ds(odd_at, halo)], sem.at[1]),
    ]
    return copies, odd_at


def fence(plane, planes, odd_at, halo, field):
    @pl.when((plane == 0) | (plane == planes - 1))
    def _():
        for t in range(field.shape[0]):
            field[t, pl.ds(odd_at, halo)] = jnp.full((halo, LANES), far_value, jnp.float32)


def first_kernel(count, sweeps, has_cost, planes, p0, p1, p2, p3, even, odd, *rest):
    if has_cost:
        state, low_ref, high_ref, cost_out, one, two, cost, sem = rest
    else:
        cost_in, state, low_ref, high_ref, one, two, cost, sem = rest
    member, plane, _ = here()
    rows, halo = p0.shape[1], even.shape[1]
    total = PLANE * rows
    tiles = cost.shape[1]
    size = count * tiles
    base = cost.at[0]
    copies, sems = [], 16
    for s in range(count):
        slabs = slice(s * tiles, (s + 1) * tiles)
        for j, p in enumerate((p0, p1, p2, p3)):
            at = pl.multiple_of(PAD + halo + (member ^ j) * rows, 8)
            copies.append(
                pltpu.make_async_copy(
                    p.at[slabs], core(one, s, tiles).at[:, pl.ds(at, rows)], sem.at[sems]
                )
            )
            sems += 1
        halos, odd_at = halo_copies(
            plane, halo, total, even, odd, core(one, s, tiles), sem.at[pl.ds(sems, 2)], slabs
        )
        copies += halos
        sems += 2
    if has_cost:
        more, _ = halo_copies(
            plane, halo, total, even, odd, base, sem.at[pl.ds(2, 2)], slice(size, size + tiles)
        )
        copies += more
        copies += [
            pltpu.make_async_copy(
                p.at[size : size + tiles],
                base.at[:, pl.ds(pl.multiple_of(PAD + halo + (member ^ j) * rows, 8), rows)],
                sem.at[8 + j],
            )
            for j, p in enumerate((p0, p1, p2, p3))
        ]
    else:
        copies.append(pltpu.make_async_copy(cost_in, cost, sem.at[8]))
    run_copies(copies)
    for s in range(count):
        fence(plane, planes, odd_at, halo, core(one, s, tiles))
    if has_cost:
        fence(plane, planes, odd_at, halo, base)
        scale_cost(cost)
    run_sweeps(one, two, cost, count, tiles, sweeps)
    parity = lax.rem(plane, 2)
    top, bottom = PAD + halo, PAD + halo + total - halo
    low = pl.multiple_of(parity * top + (1 - parity) * bottom, 8)
    high = pl.multiple_of((1 - parity) * top + parity * bottom, 8)
    copies = []
    for s in range(count):
        slabs = slice(s * tiles, (s + 1) * tiles)
        for k, (at, size_at, out) in enumerate(
            ((low, halo, low_ref), (high, halo, high_ref), (PAD + halo, total, state))
        ):
            copies.append(
                pltpu.make_async_copy(
                    core(one, s, tiles).at[:, pl.ds(at, size_at)],
                    out.at[slabs],
                    sem.at[16 + 3 * s + k],
                )
            )
    if has_cost:
        copies.append(pltpu.make_async_copy(cost, cost_out, sem.at[3]))
    run_copies(copies)


def last_kernel(count, sweeps, is_last, planes, cap, state, even, odd, cost_in, m0, m1, m2, m3, *rest):
    if is_last:
        partial_ref, earlier_ref, placed_ref, r0, r1, r2, r3, one, two, cost, meta, best, plain, sem = rest
    else:
        placed_ref, best, one, two, cost, meta, sem = rest
    member, plane, _ = here()
    total, halo = state.shape[1], even.shape[1]
    rows = total // PLANE
    tiles = cost.shape[1]
    own = tiles - 1
    copies = [pltpu.make_async_copy(cost_in, cost, sem.at[3])]
    for s in range(count):
        slabs = slice(s * tiles, (s + 1) * tiles)
        inner = core(one, s, tiles)
        copies.append(
            pltpu.make_async_copy(
                state.at[slabs], inner.at[:, PAD + halo : PAD + halo + total], sem.at[8 + 3 * s]
            )
        )
        halos, odd_at = halo_copies(
            plane, halo, total, even, odd, inner, sem.at[pl.ds(9 + 3 * s, 2)], slabs
        )
        copies += halos
    copies += [
        pltpu.make_async_copy(m.at[m.shape[0] - 1], meta.at[member ^ j], sem.at[4 + j])
        for j, m in enumerate((m0, m1, m2, m3))
    ]
    run_copies(copies)
    for s in range(count):
        fence(plane, planes, odd_at, halo, core(one, s, tiles))
    run_sweeps(one, two, cost, count, tiles, sweeps)

    for t in range(tiles):
        low = None
        for s in range(count):
            at = (s, REACH + t, slice(PAD + halo, PAD + halo + total))
            each = jnp.minimum(one[at], jnp.float32(clip_value)) / clip_value
            one[at] = each
            low = each if low is None else jnp.minimum(low, each)
        best[t] = jnp.minimum(low, partial_ref[t]) if is_last else low
    copies = []
    if is_last:
        lane = lax.broadcasted_iota(jnp.int32, (8, LANES), 1)
        orders = [((lane + (LANES - j)) * inverse(tiles)) & (LANES - 1) for j in range(tiles)]
        chosen = [lax.rem(lane + t * LANES, tiles) for t in range(own)]

        def back(at, carry):
            spot = pl.ds(pl.multiple_of(at * 8, 8), 8)
            turned = [gather_lanes(best[j, spot], orders[j]) for j in range(tiles)]
            for t in range(own):
                value = turned[0]
                for j in range(1, tiles):
                    value = jnp.where(chosen[t] == j, turned[j], value)
                plain[t, spot] = value
            return carry

        lax.fori_loop(0, total // 8, back, 0)
        copies = [
            pltpu.make_async_copy(
                plain.at[:, pl.ds(pl.multiple_of((member ^ j) * rows, 8), rows)], r, sem.at[j]
            )
            for j, r in enumerate((r0, r1, r2, r3))
        ]
        for copy in copies:
            copy.start()

    def exact(pick, value):
        found = None
        for _ in range(3):
            part = value.astype(jnp.bfloat16)
            value = value - part.astype(jnp.float32)
            term = jnp.dot(pick, part, preferred_element_type=jnp.float32)
            found = term if found is None else found + term
        return found

    n, _, slots = placed_ref.shape
    height = tiles * rows
    lane = lax.broadcasted_iota(jnp.int32, (LANES, LANES), 1).astype(jnp.float32)
    place = lax.broadcasted_iota(jnp.int32, (LANES, height), 1).astype(jnp.float32)
    spot = lax.broadcasted_iota(jnp.int32, (LANES, slots), 1).astype(jnp.float32)
    device = lax.broadcasted_iota(jnp.int32, (n, LANES), 0).astype(jnp.float32)
    filler = jnp.zeros((LANES - meta.shape[1], LANES), jnp.float32)
    offset = (member * height).astype(jnp.float32)
    totals = [None] * count
    for q in range(PLANE):
        turned = jnp.transpose(jnp.concatenate([meta[q], filler], axis=0))
        pick = jnp.where(turned[:, 0:1] - offset == place, 1.0, 0.0).astype(jnp.bfloat16)
        at_lane = turned[:, 1:2] == lane
        base = ((plane * PLANE + q) * cap).astype(jnp.float32)
        at_slot = turned[:, 3:4] + base == spot
        to_owner = jnp.where(meta[q, 2:3] == device, 1.0, 0.0).astype(jnp.bfloat16)
        for s in range(count):
            block = one[s, REACH : REACH + tiles, PAD + halo + q * rows : PAD + halo + (q + 1) * rows]
            found = exact(pick, block.reshape(height, LANES))
            value = jnp.sum(jnp.where(at_lane, found, 0.0), axis=1, keepdims=True)
            term = exact(to_owner, jnp.where(at_slot, value, 0.0))
            totals[s] = term if totals[s] is None else totals[s] + term
    if is_last:
        placed_ref[:, 0:count] = earlier_ref[...]
        for s in range(count):
            placed_ref[:, count + s] = totals[s]
    else:
        for s in range(count):
            placed_ref[:, s] = totals[s]
    for copy in copies:
        copy.wait()


def join_kernel(r0, r1, r2, r3, gauge_ref, out_ref, result_ref):
    member, _, _ = here()
    tiles, rows, _ = r0.shape
    for j, r in enumerate((r0, r1, r2, r3)):
        base = (member ^ j) * (tiles * LANES)
        for t in range(tiles):
            out_ref[:, pl.ds(pl.multiple_of(base + t * LANES, LANES), LANES)] = r[t]
    result_ref[0] = jnp.sum(gauge_ref[...], axis=0)


def shape_of(*dims):
    return jax.ShapeDtypeStruct(dims, jnp.float32)


def on_device(slowness, ocean, start_times, source_cells, gauge_cells, gauge_owner):
    axis = "space"
    index = lax.axis_index(axis)
    n = lax.axis_size(axis)
    rows, width = slowness.shape
    sources = start_times.shape[0]
    gauges = gauge_cells.shape[0]
    planes = n // PLANE
    assert n % (2 * PLANE) == 0 and width % (PLANE * LANES) == 0
    assert gauges == LANES and rows * (width // PLANE) == LANES * LANES and sources % 2 == 0
    sweeps = SWEEPS * BLOCKS // ROUNDS
    halo = 2 * sweeps
    total = rows * PLANE
    tiles = width // PLANE // LANES + 1
    assert 2 * SWEEPS * BLOCKS <= SIDE and halo <= total and sweeps % 2 == 0 and halo % 8 == 0
    cap = max(2, 2 * gauges // n)
    half = sources // 2
    groups = (tuple(range(half)), tuple(range(half, sources)))
    limit = pltpu.CompilerParams(vmem_limit_bytes=VMEM_BYTES)

    sizes = [half * tiles + tiles + 1, half * tiles]
    packed = pl.pallas_call(
        functools.partial(pack_kernel, groups, cap),
        out_shape=[shape_of(size, rows, LANES) for size in sizes for _ in range(PLANE)],
        in_specs=[SMEM, VMEM, VMEM, VMEM, VMEM, VMEM],
        out_specs=[ANY] * (2 * PLANE),
        scratch_shapes=[
            pltpu.VMEM((PLANE, sources + 1, tiles, rows + 8, LANES), jnp.float32),
            pltpu.VMEM((PLANE, sum(sizes), rows, LANES), jnp.float32),
            pltpu.SemaphoreType.DMA((2 * PLANE,)),
        ],
        name="pack",
        compiler_params=limit,
    )(
        source_cells,
        slowness,
        ocean,
        start_times,
        gauge_cells.reshape(1, gauges),
        gauge_owner.reshape(1, gauges),
    )

    def swap(x, j):
        return lax.ppermute(x, axis, [(d, d ^ j) for d in range(n)])

    def swap_planes(even, odd):
        pairs_even = [(d, (d // PLANE ^ 1) * PLANE + d % PLANE) for d in range(n)]
        pairs_odd = [
            (d, (((d // PLANE + 1) ^ 1) - 1) * PLANE + d % PLANE)
            for d in range(PLANE, n - PLANE)
        ]
        return lax.ppermute(even, axis, pairs_even), lax.ppermute(odd, axis, pairs_odd)

    pieces = [
        [packed[k * PLANE]] + [swap(packed[k * PLANE + j], j) for j in range(1, PLANE)]
        for k in range(2)
    ]
    halos = []
    for k in range(2):
        slabs = half * tiles + (tiles if k == 0 else 0)
        even, odd = pl.pallas_call(
            functools.partial(edge_kernel, slabs, halo),
            out_shape=[shape_of(slabs, halo, LANES)] * 2,
            in_specs=[ANY] * 4,
            out_specs=[ANY] * 2,
            compiler_params=limit,
            scratch_shapes=[
                pltpu.VMEM((slabs, total, LANES), jnp.float32),
                pltpu.SemaphoreType.DMA((PLANE,)),
            ],
            name=f"edge{k}",
        )(*pieces[k])
        halos.append(swap_planes(even, odd))

    deep = total + 2 * halo + 3 * PAD
    size = half * tiles
    scratch = [
        pltpu.VMEM((half, tiles + 2 * REACH, deep, LANES), jnp.float32),
        pltpu.VMEM((half, tiles + 2 * REACH, deep, LANES), jnp.float32),
        pltpu.VMEM((3, tiles, deep, LANES), jnp.float32),
    ]
    states, later = [], []
    cost = None
    for k in range(2):
        outs = pl.pallas_call(
            functools.partial(first_kernel, half, sweeps, k == 0, planes),
            out_shape=[shape_of(size, total, LANES)]
            + [shape_of(size, halo, LANES)] * 2
            + ([shape_of(3, tiles, deep, LANES)] if k == 0 else []),
            in_specs=[ANY] * (6 if k == 0 else 7),
            compiler_params=limit,
            out_specs=[ANY] * (4 if k == 0 else 3),
            scratch_shapes=scratch + [pltpu.SemaphoreType.DMA((16 + 6 * half,))],
            name=f"first{k}",
        )(*pieces[k], *halos[k], *([] if k == 0 else [cost]))
        if k == 0:
            cost = outs[3]
        states.append(outs[0])
        later.append(swap_planes(outs[1], outs[2]))

    slots = n * cap
    partial, placed = None, None
    for k in range(2):
        is_last = k == 1
        out_shape = [shape_of(n, half * (k + 1), slots)]
        out_specs = [VMEM]
        more = [pltpu.VMEM((PLANE, rows, LANES), jnp.float32)]
        if is_last:
            out_shape += [shape_of(tiles - 1, rows, LANES)] * PLANE
            out_specs += [ANY] * PLANE
            more.append(pltpu.VMEM((tiles, total, LANES), jnp.float32))
            more.append(pltpu.VMEM((tiles - 1, total, LANES), jnp.float32))
        else:
            out_shape.append(shape_of(tiles, total, LANES))
            out_specs.append(VMEM)
        outs = pl.pallas_call(
            functools.partial(last_kernel, half, sweeps, is_last, planes, cap),
            out_shape=out_shape,
            in_specs=[ANY] * 8 + ([VMEM, VMEM] if is_last else []),
            out_specs=out_specs,
            scratch_shapes=scratch + more + [pltpu.SemaphoreType.DMA((8 + 3 * half,))],
            compiler_params=limit,
            name=f"last{k}",
        )(states[k], *later[k], cost, *pieces[0], *([partial, placed] if is_last else []))
        placed = outs[0]
        if is_last:
            returned = outs[1:]
        else:
            partial = outs[1]

    back = [returned[0]] + [swap(returned[j], j) for j in range(1, PLANE)]
    received = lax.all_to_all(placed, axis, split_axis=0, concat_axis=0, tiled=True)
    return pl.pallas_call(
        join_kernel,
        out_shape=(shape_of(rows, width), shape_of(1, sources, slots)),
        in_specs=[VMEM] * (PLANE + 1),
        out_specs=(VMEM, VMEM),
        compiler_params=limit,
        name="join",
    )(*back, received)


def solution(mesh):
    return jax.shard_map(
        on_device,
        mesh=mesh,
        in_specs=(
            P(("groups", "space"), None),
            P(("groups", "space"), None),
            P("groups", "space", None),
            P("groups"),
            P(("groups", "space")),
            P(("groups", "space"), None),
        ),
        out_specs=(P(("groups", "space"), None), P(("groups", "space"), None, None)),
        check_vma=False,
    )
```

```python
import functools
import jax
import jax.numpy as jnp
from jax import lax
from jax.experimental import pallas as pl
from jax.experimental.pallas import tpu as pltpu
from jax.sharding import PartitionSpec as P

SWEEPS = 8
BLOCKS = 3
FIRST = 8

far_value = 1000000.0
land_cost = 10000.0
clip_value = 48.0
root_two = 1.41421356
root_five = 2.23606798

PLANE = 4
LANES = 128
SIDE = 64
PAD = 8
REACH = 2
VMEM_BYTES = 24 * 1024 * 1024
ANY = pl.BlockSpec(memory_space=pl.ANY)
HBM = pl.BlockSpec(memory_space=pltpu.HBM)
SMEM = pl.BlockSpec(memory_space=pltpu.SMEM)
VMEM = pl.BlockSpec(memory_space=pltpu.VMEM)


def run_copies(copies):
    def each(act):
        for copy in copies:
            if isinstance(copy, tuple):
                pl.when(copy[0])(functools.partial(act, copy[1]))
            else:
                act(copy)

    each(lambda copy: copy.start())
    each(lambda copy: copy.wait())


class Semaphores:
    def __init__(self, sem):
        self.sem, self.used = sem, 0

    def copy(self, source, target):
        self.used += 1
        return pltpu.make_async_copy(source, target, self.sem.at[self.used - 1])


def inverse(number):
    return pow(number, -1, LANES)


def gather_lanes(x, order):
    return jnp.take_along_axis(x, order, axis=1, mode="promise_in_bounds")


def here():
    index = lax.axis_index("space")
    return lax.rem(index, PLANE), lax.div(index, PLANE), index


def aligned(at):
    return pl.multiple_of(at, 8)


def pack_kernel(groups, source_hbm, slow_hbm, ocean_hbm, start_hbm, cell_hbm, owner_hbm, *rest):
    outs, (source_ref, cell_ref, owner_ref, field_ref, ocean_ref, side_ref, sem) = rest[:-7], rest[-7:]
    sources, rows, width = start_hbm.shape
    own = width // PLANE
    tiles = own // LANES
    chunk = tiles + 1
    member, _, index = here()
    sems = Semaphores(sem)
    run_copies(
        [
            sems.copy(start_hbm, field_ref.at[0:sources]),
            sems.copy(slow_hbm, field_ref.at[sources]),
            sems.copy(ocean_hbm, ocean_ref),
            sems.copy(source_hbm, source_ref),
            sems.copy(cell_hbm, cell_ref),
            sems.copy(owner_hbm, owner_ref),
        ]
    )
    lane = lax.broadcasted_iota(jnp.int32, (8, LANES), 1)
    row = lax.broadcasted_iota(jnp.int32, (8, LANES), 0)
    far = jnp.full((8, LANES), far_value, jnp.float32)

    for t in range(width // LANES):
        at = slice(t * LANES, (t + 1) * LANES)
        field_ref[sources, :, at] = jnp.where(
            ocean_ref[:, at] == 1, field_ref[sources, :, at], jnp.float32(land_cost)
        )
    for s in range(sources):
        cell = source_ref[s] - index * (rows * width)

        @pl.when((cell >= 0) & (cell < rows * width))
        def _():
            line, column = lax.div(cell, width), lax.rem(cell, width)
            spot = pl.ds(aligned(lax.div(line, 8) * 8), 8)
            at = pl.ds(pl.multiple_of(lax.div(column, LANES) * LANES, LANES), LANES)
            hit = (row == lax.rem(line, 8)) & (lane == lax.rem(column, LANES))
            field_ref[s, spot, at] = jnp.where(hit, 0.0, field_ref[s, spot, at])

    for f in range(sources + 1):
        for w in range(PLANE):
            for half in range(0, rows, 8):
                right = (w + 1) * own
                left = w * own - LANES
                value_right = field_ref[f, half : half + 8, right : right + LANES] if w < PLANE - 1 else far
                value_left = field_ref[f, half : half + 8, left : left + LANES] if w > 0 else far
                side_ref[w, f, half : half + 8] = jnp.where(lane < SIDE, value_right, value_left)

    order_of = []
    for number, group in enumerate(groups):
        order_of += [(number, k, s) for k, s in enumerate(group)]
        if number == 0:
            order_of.append((0, len(group), sources))

    def convert(j, carry):
        column = (((lane + (LANES - j)) * inverse(chunk)) & (LANES - 1)) * chunk + j
        masks = [column >= t * LANES for t in range(1, chunk)]
        order = (lane * chunk + j) & (LANES - 1)
        for shift in range(PLANE):
            window = member ^ shift
            for number, slab, f in order_of:
                out = outs[number * PLANE + shift]
                for half in range(0, rows, 8):
                    mixed = None
                    for t in range(chunk):
                        if t < tiles:
                            at = pl.multiple_of(window * own + t * LANES, LANES)
                            value = field_ref[f, half : half + 8, pl.ds(at, LANES)]
                        else:
                            value = side_ref[window, f, half : half + 8]
                        mixed = value if t == 0 else jnp.where(masks[t - 1], value, mixed)
                    out[slab * chunk + j, half : half + 8] = gather_lanes(mixed, order)
        return carry

    lax.fori_loop(0, chunk, convert, 0)

    owner = owner_ref[...].astype(jnp.float32)
    across = jnp.broadcast_to(owner, (LANES, LANES))
    down = jnp.transpose(across)
    earlier = lax.broadcasted_iota(jnp.int32, (LANES, LANES), 0) < lax.broadcasted_iota(
        jnp.int32, (LANES, LANES), 1
    )
    rank = jnp.sum(jnp.where(earlier & (across == down), 1.0, 0.0), axis=0, keepdims=True)
    cell = cell_ref[...].astype(jnp.float32)
    line = jnp.floor(cell / width)
    column = cell - line * width
    part = jnp.floor(column / own)
    column = column - part * own
    spot = jnp.floor((column + 0.5) / chunk)
    place = (part * chunk + (column - spot * chunk)) * rows + line
    filler = jnp.zeros((rows - 4, LANES), jnp.float32)
    meta = jnp.concatenate([place, spot, owner, rank, filler], axis=0)
    for shift in range(PLANE):
        outs[shift][outs[shift].shape[0] - 1] = meta


def keep_ends(dst, s, t, spot, value, tiles):
    if t < REACH:
        dst[s, tiles + REACH + t, spot] = pltpu.roll(value, LANES - 1, 1)
    if t >= tiles - REACH:
        dst[s, t - (tiles - REACH), spot] = pltpu.roll(value, 1, 1)


def relax_rows(src, dst, cost, count, tiles, start):
    spot = pl.ds(start, 8)
    order = sorted(range(tiles), key=lambda t: REACH <= t < tiles - REACH)
    for s in range(count):

        def load(t, shift):
            return src[s, t + REACH, pl.ds(start + shift, 8)]

        near = {t: load(t, 0) for t in range(-1, tiles + 1)}
        one = {t: jnp.minimum(load(t, -1), load(t, 1)) for t in range(-2, tiles + 2)}
        two = {t: jnp.minimum(load(t, -2), load(t, 2)) for t in range(-1, tiles + 1)}
        for t in order:
            m1 = jnp.minimum(one[t], jnp.minimum(near[t - 1], near[t + 1]))
            m2 = jnp.minimum(one[t - 1], one[t + 1])
            m5 = jnp.minimum(
                jnp.minimum(one[t - 2], one[t + 2]), jnp.minimum(two[t - 1], two[t + 1])
            )
            best = jnp.minimum(m1 + cost[0, t, spot], m2 + cost[1, t, spot])
            best = jnp.minimum(best, m5 + cost[2, t, spot])
            value = jnp.minimum(near[t], best)
            dst[s, t + REACH, spot] = value


def fill_rows(field, tiles, start):
    spot = pl.ds(start, 8)
    for s in range(field.shape[0]):
        for t in list(range(REACH)) + list(range(tiles - REACH, tiles)):
            keep_ends(field, s, t, spot, field[s, t + REACH, spot], tiles)


def fill_ends(field, tiles):
    def group(at, carry):
        for k in range(2):
            fill_rows(field, tiles, pl.multiple_of(PAD + at * 16 + k * 8, 8))
        return carry

    lax.fori_loop(0, (field.shape[2] - 3 * PAD) // 16, group, 0)


def scale_cost(cost):
    def group(at, carry):
        spot = pl.ds(pl.multiple_of(at * 8, 8), 8)
        for t in range(cost.shape[1]):
            value = cost[0, t, spot]
            cost[1, t, spot] = root_two * value
            cost[2, t, spot] = root_five * value
        return carry

    lax.fori_loop(0, cost.shape[2] // 8, group, 0)


def run_sweeps(first, second, cost, count, tiles, sweeps, groups):
    def sweep(src, dst, number):
        low = lax.shift_right_logical(number, 2)

        def group(at, carry):
            start = aligned(PAD + (low + 2 * at) * 8)
            fill_rows(dst, tiles, aligned(start - 8))
            relax_rows(src, dst, cost, count, tiles, start)
            fill_rows(dst, tiles, start)
            relax_rows(src, dst, cost, count, tiles, aligned(start + 8))
            return carry

        lax.fori_loop(0, groups // 2 - low, group, 0)
        fill_rows(dst, tiles, aligned(PAD + (groups - low - 1) * 8))

    def pair(at, carry):
        sweep(first, second, 2 * at + 1)
        sweep(second, first, 2 * at + 2)
        return carry

    fill_ends(first, tiles)
    lax.fori_loop(0, sweeps // 2, pair, 0)


def core(field, s, tiles):
    return field.at[s, REACH : REACH + tiles]


def fence(plane, planes, halo, total, field):
    for missing, at in ((plane == 0, PAD), (plane == planes - 1, PAD + halo + total)):

        @pl.when(missing)
        def _():
            for t in range(field.shape[0]):
                field[t, at : at + halo] = jnp.full((halo, LANES), far_value, jnp.float32)


def first_kernel(count, halo, planes, edge, has_cost, *refs):
    own, beside, rest = refs[0:4], refs[4:8], refs[8:]
    if has_cost:
        state, low_ref, high_ref, cost_out, one, two, cost, sem = rest
    else:
        cost_in, state, low_ref, high_ref, one, two, cost, sem = rest
    member, plane, _ = here()
    rows = own[0].shape[1]
    total = PLANE * rows
    tiles = cost.shape[1]
    sems = Semaphores(sem)

    def gather(slabs, field):
        copies = []
        for j in range(PLANE):
            at = aligned(PAD + halo + (member ^ j) * rows)
            copies.append(sems.copy(own[j].at[slabs], field.at[:, pl.ds(at, rows)]))
            below = sems.copy(beside[j].at[slabs], field.at[:, PAD + halo + total : PAD + total + 2 * halo])
            above = sems.copy(beside[j].at[slabs], field.at[:, PAD : PAD + halo])
            copies.append(((member == j) & (plane < planes - 1), below))
            copies.append(((member == PLANE - 1 - j) & (plane > 0), above))
        return copies

    copies = []
    for s in range(count):
        copies += gather(slice(s * tiles, (s + 1) * tiles), core(one, s, tiles))
    if has_cost:
        copies += gather(slice(count * tiles, (count + 1) * tiles), cost.at[0])
    else:
        copies.append(sems.copy(cost_in, cost))
    run_copies(copies)
    for s in range(count):
        fence(plane, planes, halo, total, core(one, s, tiles))
    if has_cost:
        fence(plane, planes, halo, total, cost.at[0])
        scale_cost(cost)
    run_sweeps(one, two, cost, count, tiles, FIRST, (total + 2 * halo) // 8)
    parity = lax.rem(plane, 2)
    top, bottom = PAD + halo, PAD + halo + total - edge
    low = aligned(parity * top + (1 - parity) * bottom)
    high = aligned((1 - parity) * top + parity * bottom)
    fields = [core(one, s, tiles) for s in range(count)] + ([cost.at[0]] if has_cost else [])
    copies = []
    for k, field in enumerate(fields):
        slabs = slice(k * tiles, (k + 1) * tiles)
        copies.append(sems.copy(field.at[:, pl.ds(low, edge)], low_ref.at[slabs]))
        copies.append(sems.copy(field.at[:, pl.ds(high, edge)], high_ref.at[slabs]))
        copies.append(sems.copy(field.at[:, PAD + halo : PAD + halo + total], state.at[slabs]))
    if has_cost:
        copies.append(sems.copy(cost, cost_out))
    run_copies(copies)


def last_kernel(count, sweeps, is_last, planes, state, even, odd, base, base_even, base_odd, *rest):
    if is_last:
        partial_ref, each_ref, r0, r1, r2, r3, one, two, cost, best, plain, sem = rest
    else:
        each_ref, best, one, two, cost, sem = rest
    member, plane, _ = here()
    total, halo = state.shape[1], even.shape[1]
    rows = total // PLANE
    tiles = cost.shape[1]
    own = tiles - 1
    sems = Semaphores(sem)
    parity = lax.rem(plane, 2)
    above, below = PAD, PAD + halo + total
    even_at = aligned(parity * above + (1 - parity) * below)
    odd_at = aligned((1 - parity) * above + parity * below)

    def gather(slabs, field, middle, from_even, from_odd):
        return [
            sems.copy(middle.at[slabs], field.at[:, PAD + halo : PAD + halo + total]),
            sems.copy(from_even.at[slabs], field.at[:, pl.ds(even_at, halo)]),
            sems.copy(from_odd.at[slabs], field.at[:, pl.ds(odd_at, halo)]),
        ]

    copies = gather(slice(count * tiles, (count + 1) * tiles), cost.at[0], base, base_even, base_odd)
    for s in range(count):
        copies += gather(slice(s * tiles, (s + 1) * tiles), core(one, s, tiles), state, even, odd)
    run_copies(copies)
    for s in range(count):
        fence(plane, planes, halo, total, core(one, s, tiles))
    fence(plane, planes, halo, total, cost.at[0])
    scale_cost(cost)
    run_sweeps(one, two, cost, count, tiles, sweeps, (total + 2 * halo) // 8)

    for t in range(tiles):
        low = None
        for s in range(count):
            each = jnp.minimum(
                one[s, REACH + t, PAD + halo : PAD + halo + total], jnp.float32(clip_value)
            )
            each = each / clip_value
            each_ref[s * tiles + t] = each
            low = each if low is None else jnp.minimum(low, each)
        best[t] = jnp.minimum(low, partial_ref[t]) if is_last else low
    if not is_last:
        return
    lane = lax.broadcasted_iota(jnp.int32, (8, LANES), 1)
    orders = [((lane + (LANES - j)) * inverse(tiles)) & (LANES - 1) for j in range(tiles)]
    chosen = [lax.rem(lane + t * LANES, tiles) for t in range(own)]

    def back(at, carry):
        spot = pl.ds(aligned(at * 8), 8)
        turned = [gather_lanes(best[j, spot], orders[j]) for j in range(tiles)]
        for t in range(own):
            value = turned[0]
            for j in range(1, tiles):
                value = jnp.where(chosen[t] == j, turned[j], value)
            plain[t, spot] = value
        return carry

    lax.fori_loop(0, total // 8, back, 0)
    run_copies(
        [
            sems.copy(plain.at[:, pl.ds(aligned((member ^ j) * rows), rows)], r)
            for j, r in enumerate((r0, r1, r2, r3))
        ]
    )


def gauge_kernel(cap, half, each_a, each_b, m0, m1, m2, m3, placed_ref, meta, sem):
    def exact(pick, value):
        found = None
        for _ in range(3):
            part = value.astype(jnp.bfloat16)
            value = value - part.astype(jnp.float32)
            term = jnp.dot(pick, part, preferred_element_type=jnp.float32)
            found = term if found is None else found + term
        return found

    member, plane, _ = here()
    sems = Semaphores(sem)
    run_copies(
        [
            sems.copy(m.at[m.shape[0] - 1], meta.at[member ^ j])
            for j, m in enumerate((m0, m1, m2, m3))
        ]
    )
    n, sources, slots = placed_ref.shape
    rows = each_a.shape[1] // PLANE
    tiles = each_a.shape[0] // half
    height = tiles * rows
    lane = lax.broadcasted_iota(jnp.int32, (LANES, LANES), 1).astype(jnp.float32)
    place = lax.broadcasted_iota(jnp.int32, (LANES, height), 1).astype(jnp.float32)
    spot = lax.broadcasted_iota(jnp.int32, (LANES, slots), 1).astype(jnp.float32)
    device = lax.broadcasted_iota(jnp.int32, (n, LANES), 0).astype(jnp.float32)
    filler = jnp.zeros((LANES - meta.shape[1], LANES), jnp.float32)
    offset = (member * height).astype(jnp.float32)
    placed_ref[...] = jnp.zeros(placed_ref.shape, jnp.float32)

    def block_of(q, carry):
        turned = jnp.transpose(jnp.concatenate([meta[q], filler], axis=0))
        pick = jnp.where(turned[:, 0:1] - offset == place, 1.0, 0.0).astype(jnp.bfloat16)
        at_lane = turned[:, 1:2] == lane
        base = ((plane * PLANE + q) * cap).astype(jnp.float32)
        at_slot = turned[:, 3:4] + base == spot
        to_owner = jnp.where(meta[q, 2:3] == device, 1.0, 0.0).astype(jnp.bfloat16)
        blocks = []
        for s in range(sources):
            each, k = (each_a, s) if s < half else (each_b, s - half)
            block = each[k * tiles : (k + 1) * tiles, pl.ds(aligned(q * rows), rows)]
            blocks.append(block.reshape(height, LANES))
        found = exact(pick, jnp.concatenate(blocks, axis=1))
        for s in range(sources):
            mine = jnp.where(at_lane, found[:, s * LANES : (s + 1) * LANES], 0.0)
            value = jnp.sum(mine, axis=1, keepdims=True)
            placed_ref[:, s] = placed_ref[:, s] + exact(to_owner, jnp.where(at_slot, value, 0.0))
        return carry

    lax.fori_loop(0, PLANE, block_of, 0)


def join_kernel(r0, r1, r2, r3, gauge_ref, out_ref, result_ref):
    member, _, _ = here()
    tiles, _, _ = r0.shape
    for j, r in enumerate((r0, r1, r2, r3)):
        base = (member ^ j) * (tiles * LANES)
        for t in range(tiles):
            out_ref[:, pl.ds(pl.multiple_of(base + t * LANES, LANES), LANES)] = r[t]
    result_ref[0] = jnp.sum(gauge_ref[...], axis=0)


def shape_of(*dims):
    return jax.ShapeDtypeStruct(dims, jnp.float32)


def on_device(slowness, ocean, start_times, source_cells, gauge_cells, gauge_owner):
    axis = "space"
    n = lax.axis_size(axis)
    rows, width = slowness.shape
    sources = start_times.shape[0]
    gauges = gauge_cells.shape[0]
    planes = n // PLANE
    later_sweeps = SWEEPS * BLOCKS - FIRST
    halo, edge = 2 * FIRST, 2 * later_sweeps
    total = rows * PLANE
    tiles = width // PLANE // LANES + 1
    assert n % (2 * PLANE) == 0 and width % (PLANE * LANES) == 0 and tiles % 2 == 1
    assert gauges == LANES and sources % 2 == 0 and rows == halo
    assert 2 * SWEEPS * BLOCKS <= SIDE and edge <= total and FIRST % 2 == later_sweeps % 2 == 0
    assert total % 16 == halo % 8 == edge % 8 == 0
    cap = max(2, 2 * gauges // n)
    half = sources // 2
    groups = (tuple(range(half)), tuple(range(half, sources)))
    size = half * tiles
    sizes = [size + tiles + 1, size]

    def call(kernel, out_shape, in_specs, out_specs, scratch, micros=2):
        return pl.pallas_call(
            kernel,
            out_shape=out_shape,
            in_specs=in_specs,
            out_specs=out_specs,
            scratch_shapes=scratch,
            compiler_params=pltpu.CompilerParams(vmem_limit_bytes=VMEM_BYTES),
            cost_estimate=pl.CostEstimate(
                flops=0, bytes_accessed=3_000_000 * micros, transcendentals=0
            ),
        )

    def vmem(*dims):
        return pltpu.VMEM(dims, jnp.float32)

    def semaphores(number):
        return pltpu.SemaphoreType.DMA((number,))

    packed = call(
        functools.partial(pack_kernel, groups),
        [shape_of(k, rows, LANES) for k in sizes for _ in range(PLANE)],
        [HBM] * 6,
        [VMEM] * (2 * PLANE),
        [
            pltpu.SMEM((sources,), jnp.int32),
            pltpu.VMEM((1, gauges), jnp.int32),
            pltpu.VMEM((1, gauges), jnp.int32),
            vmem(sources + 1, rows, width),
            pltpu.VMEM((rows, width), jnp.int32),
            vmem(PLANE, sources + 1, rows, LANES),
            semaphores(6),
        ],
    )(
        *(
            pltpu.with_memory_space_constraint(x, pltpu.HBM)
            for x in (
                source_cells,
                slowness,
                ocean,
                start_times,
                gauge_cells.reshape(1, gauges),
                gauge_owner.reshape(1, gauges),
            )
        )
    )

    def swap(x, j):
        return lax.ppermute(x, axis, [(d, d ^ j) for d in range(n)])

    def to_next_planes(x, j):
        up = [(z * PLANE, (z - 1) * PLANE + j) for z in range(1, planes)]
        down = [(z * PLANE + PLANE - 1, (z + 1) * PLANE + (PLANE - 1 - j)) for z in range(planes - 1)]
        return lax.ppermute(x, axis, up + down)

    def swap_planes(even, odd):
        pairs_even = [(d, (d // PLANE ^ 1) * PLANE + d % PLANE) for d in range(n)]
        pairs_odd = [
            (d, (((d // PLANE + 1) ^ 1) - 1) * PLANE + d % PLANE)
            for d in range(PLANE, n - PLANE)
        ]
        return lax.ppermute(even, axis, pairs_even), lax.ppermute(odd, axis, pairs_odd)

    pieces, beside = [], []
    for k in range(2):
        mine = packed[k * PLANE : (k + 1) * PLANE]
        pieces.append([mine[0]] + [swap(mine[j], j) for j in range(1, PLANE)])
        beside.append([to_next_planes(mine[j], j) for j in range(PLANE)])

    def buffers(deep):
        deep += 3 * PAD
        ends = tiles + 2 * REACH
        return [vmem(half, ends, deep, LANES), vmem(half, ends, deep, LANES), vmem(3, tiles, deep, LANES)]

    states, later, cost = [], [], None
    for k in range(2):
        slabs = size + (tiles if k == 0 else 0)
        scratch = buffers(total + 2 * halo)
        outs = call(
            functools.partial(first_kernel, half, halo, planes, edge, k == 0),
            [shape_of(slabs, total, LANES)]
            + [shape_of(slabs, edge, LANES)] * 2
            + ([shape_of(*scratch[2].shape)] if k == 0 else []),
            [ANY] * (2 * PLANE + k),
            [ANY] * (4 - k),
            scratch + [semaphores(3 * PLANE * (half + 1) + 3 * half + 4)],
            7,
        )(*pieces[k], *beside[k], *([] if k == 0 else [cost]))
        if k == 0:
            cost = outs[3]
        states.append(outs[0])
        later.append(swap_planes(outs[1], outs[2]))

    slots = n * cap
    each, partial = [], None
    for k in range(2):
        out_shape, out_specs, more = [shape_of(size, total, LANES)], [VMEM], []
        if k == 0:
            out_shape.append(shape_of(tiles, total, LANES))
            out_specs.append(VMEM)
        else:
            out_shape += [shape_of(tiles - 1, rows, LANES)] * PLANE
            out_specs += [ANY] * PLANE
            more = [vmem(tiles, total, LANES), vmem(tiles - 1, total, LANES)]
        outs = call(
            functools.partial(last_kernel, half, later_sweeps, k == 1, planes),
            out_shape,
            [ANY] * 6 + [VMEM] * k,
            out_specs,
            buffers(total + 2 * edge) + more + [semaphores(3 * (half + 1) + PLANE)],
            15,
        )(states[k], *later[k], states[0], *later[0], *([] if k == 0 else [partial]))
        each.append(outs[0])
        if k == 0:
            partial = outs[1]
        else:
            returned = outs[1:]

    back = [returned[0]] + [swap(returned[j], j) for j in range(1, PLANE)]
    gauge_call = call(
        functools.partial(gauge_kernel, cap, half),
        shape_of(n, sources, slots),
        [VMEM] * 2 + [ANY] * PLANE,
        VMEM,
        [vmem(PLANE, rows, LANES), semaphores(PLANE)],
        4,
    )
    placed = gauge_call(*each, *pieces[0])
    received = lax.all_to_all(placed, axis, split_axis=0, concat_axis=0, tiled=True)
    return call(
        join_kernel,
        (shape_of(rows, width), shape_of(1, sources, slots)),
        [VMEM] * (PLANE + 1),
        (VMEM, VMEM),
        [],
    )(*back, received)


def solution(mesh):
    return jax.shard_map(
        on_device,
        mesh=mesh,
        in_specs=(
            P(("groups", "space"), None),
            P(("groups", "space"), None),
            P("groups", "space", None),
            P("groups"),
            P(("groups", "space")),
            P(("groups", "space"), None),
        ),
        out_specs=(P(("groups", "space"), None), P(("groups", "space"), None, None)),
        check_vma=False,
    )
```

```python
import functools
import jax
import jax.numpy as jnp
from jax import lax
from jax.experimental import pallas as pl
from jax.experimental.pallas import tpu as pltpu
from jax.sharding import PartitionSpec as P

SWEEPS = 8
BLOCKS = 3
FIRST = 8

far_value = 1000000.0
land_cost = 10000.0
clip_value = 48.0
root_two = 1.41421356
root_five = 2.23606798

PLANE = 4
LANES = 128
SIDE = 64
PAD = 8
REACH = 2
VMEM_BYTES = 24 * 1024 * 1024
ANY = pl.BlockSpec(memory_space=pl.ANY)
HBM = pl.BlockSpec(memory_space=pltpu.HBM)
SMEM = pl.BlockSpec(memory_space=pltpu.SMEM)
VMEM = pl.BlockSpec(memory_space=pltpu.VMEM)


def run_copies(copies):
    def each(act):
        for copy in copies:
            if isinstance(copy, tuple):
                pl.when(copy[0])(functools.partial(act, copy[1]))
            else:
                act(copy)

    each(lambda copy: copy.start())
    each(lambda copy: copy.wait())


class Semaphores:
    def __init__(self, sem):
        self.sem, self.used = sem, 0

    def copy(self, source, target):
        self.used += 1
        return pltpu.make_async_copy(source, target, self.sem.at[self.used - 1])


def inverse(number):
    return pow(number, -1, LANES)


def gather_lanes(x, order):
    return jnp.take_along_axis(x, order, axis=1, mode="promise_in_bounds")


def here():
    index = lax.axis_index("space")
    return lax.rem(index, PLANE), lax.div(index, PLANE), index


def aligned(at):
    return pl.multiple_of(at, 8)


def pack_kernel(group, has_cost, source_hbm, start_hbm, *rest):
    if has_cost:
        slow_hbm, ocean_hbm, cell_hbm, owner_hbm, *outs = rest[:-7]
        source_ref, cell_ref, owner_ref, field_ref, ocean_ref, side_ref, sem = rest[-7:]
    else:
        outs = rest[:-4]
        source_ref, field_ref, side_ref, sem = rest[-4:]
    _, rows, width = start_hbm.shape
    sources = len(group)
    fields = field_ref.shape[0]
    own = width // PLANE
    tiles = own // LANES
    chunk = tiles + 1
    member, _, index = here()
    sems = Semaphores(sem)
    copies = [
        sems.copy(start_hbm.at[group[0] : group[-1] + 1], field_ref.at[0:sources]),
        sems.copy(source_hbm, source_ref),
    ]
    if has_cost:
        copies += [
            sems.copy(slow_hbm, field_ref.at[sources]),
            sems.copy(ocean_hbm, ocean_ref),
            sems.copy(cell_hbm, cell_ref),
            sems.copy(owner_hbm, owner_ref),
        ]
    run_copies(copies)
    lane = lax.broadcasted_iota(jnp.int32, (8, LANES), 1)
    row = lax.broadcasted_iota(jnp.int32, (8, LANES), 0)
    far = jnp.full((8, LANES), far_value, jnp.float32)

    for t in range(width // LANES if has_cost else 0):
        at = slice(t * LANES, (t + 1) * LANES)
        field_ref[sources, :, at] = jnp.where(
            ocean_ref[:, at] == 1, field_ref[sources, :, at], jnp.float32(land_cost)
        )
    for s in range(sources):
        cell = source_ref[group[s]] - index * (rows * width)

        @pl.when((cell >= 0) & (cell < rows * width))
        def _():
            line, column = lax.div(cell, width), lax.rem(cell, width)
            spot = pl.ds(aligned(lax.div(line, 8) * 8), 8)
            at = pl.ds(pl.multiple_of(lax.div(column, LANES) * LANES, LANES), LANES)
            hit = (row == lax.rem(line, 8)) & (lane == lax.rem(column, LANES))
            field_ref[s, spot, at] = jnp.where(hit, 0.0, field_ref[s, spot, at])

    for f in range(fields):
        for w in range(PLANE):
            for half in range(0, rows, 8):
                right = (w + 1) * own
                left = w * own - LANES
                value_right = field_ref[f, half : half + 8, right : right + LANES] if w < PLANE - 1 else far
                value_left = field_ref[f, half : half + 8, left : left + LANES] if w > 0 else far
                side_ref[w, f, half : half + 8] = jnp.where(lane < SIDE, value_right, value_left)

    def convert(j, carry):
        column = (((lane + (LANES - j)) * inverse(chunk)) & (LANES - 1)) * chunk + j
        masks = [column >= t * LANES for t in range(1, chunk)]
        order = (lane * chunk + j) & (LANES - 1)
        for shift in range(PLANE):
            window = member ^ shift
            out = outs[shift]
            for f in range(fields):
                for half in range(0, rows, 8):
                    mixed = None
                    for t in range(chunk):
                        if t < tiles:
                            at = pl.multiple_of(window * own + t * LANES, LANES)
                            value = field_ref[f, half : half + 8, pl.ds(at, LANES)]
                        else:
                            value = side_ref[window, f, half : half + 8]
                        mixed = value if t == 0 else jnp.where(masks[t - 1], value, mixed)
                    out[f * chunk + j, half : half + 8] = gather_lanes(mixed, order)
        return carry

    lax.fori_loop(0, chunk, convert, 0)
    if not has_cost:
        return

    owner = owner_ref[...].astype(jnp.float32)
    across = jnp.broadcast_to(owner, (LANES, LANES))
    down = jnp.transpose(across)
    earlier = lax.broadcasted_iota(jnp.int32, (LANES, LANES), 0) < lax.broadcasted_iota(
        jnp.int32, (LANES, LANES), 1
    )
    rank = jnp.sum(jnp.where(earlier & (across == down), 1.0, 0.0), axis=0, keepdims=True)
    cell = cell_ref[...].astype(jnp.float32)
    line = jnp.floor(cell / width)
    column = cell - line * width
    part = jnp.floor(column / own)
    column = column - part * own
    spot = jnp.floor((column + 0.5) / chunk)
    place = (part * chunk + (column - spot * chunk)) * rows + line
    filler = jnp.zeros((rows - 4, LANES), jnp.float32)
    meta = jnp.concatenate([place, spot, owner, rank, filler], axis=0)
    for shift in range(PLANE):
        outs[shift][outs[shift].shape[0] - 1] = meta


def keep_ends(dst, s, t, spot, value, tiles):
    if t < REACH:
        dst[s, tiles + REACH + t, spot] = pltpu.roll(value, LANES - 1, 1)
    if t >= tiles - REACH:
        dst[s, t - (tiles - REACH), spot] = pltpu.roll(value, 1, 1)


def relax_rows(src, dst, cost, count, tiles, start):
    spot = pl.ds(start, 8)
    order = sorted(range(tiles), key=lambda t: REACH <= t < tiles - REACH)
    for s in range(count):

        def load(t, shift):
            return src[s, t + REACH, pl.ds(start + shift, 8)]

        near = {t: load(t, 0) for t in range(-1, tiles + 1)}
        one = {t: jnp.minimum(load(t, -1), load(t, 1)) for t in range(-2, tiles + 2)}
        two = {t: jnp.minimum(load(t, -2), load(t, 2)) for t in range(-1, tiles + 1)}
        for t in order:
            m1 = jnp.minimum(one[t], jnp.minimum(near[t - 1], near[t + 1]))
            m2 = jnp.minimum(one[t - 1], one[t + 1])
            m5 = jnp.minimum(
                jnp.minimum(one[t - 2], one[t + 2]), jnp.minimum(two[t - 1], two[t + 1])
            )
            best = jnp.minimum(m1 + cost[0, t, spot], m2 + cost[1, t, spot])
            best = jnp.minimum(best, m5 + cost[2, t, spot])
            value = jnp.minimum(near[t], best)
            dst[s, t + REACH, spot] = value


def fill_rows(field, tiles, start):
    spot = pl.ds(start, 8)
    for s in range(field.shape[0]):
        for t in list(range(REACH)) + list(range(tiles - REACH, tiles)):
            keep_ends(field, s, t, spot, field[s, t + REACH, spot], tiles)


def fill_ends(field, tiles):
    def group(at, carry):
        for k in range(2):
            fill_rows(field, tiles, pl.multiple_of(PAD + at * 16 + k * 8, 8))
        return carry

    lax.fori_loop(0, (field.shape[2] - 3 * PAD) // 16, group, 0)


def scale_cost(cost):
    def group(at, carry):
        spot = pl.ds(pl.multiple_of(at * 8, 8), 8)
        for t in range(cost.shape[1]):
            value = cost[0, t, spot]
            cost[1, t, spot] = root_two * value
            cost[2, t, spot] = root_five * value
        return carry

    lax.fori_loop(0, cost.shape[2] // 8, group, 0)


def run_sweeps(first, second, cost, count, tiles, sweeps, groups):
    def sweep(src, dst, number):
        low = lax.shift_right_logical(number, 2)

        def group(at, carry):
            start = aligned(PAD + (low + 2 * at) * 8)
            fill_rows(dst, tiles, aligned(start - 8))
            relax_rows(src, dst, cost, count, tiles, start)
            fill_rows(dst, tiles, start)
            relax_rows(src, dst, cost, count, tiles, aligned(start + 8))
            return carry

        lax.fori_loop(0, groups // 2 - low, group, 0)
        fill_rows(dst, tiles, aligned(PAD + (groups - low - 1) * 8))

    def pair(at, carry):
        sweep(first, second, 2 * at + 1)
        sweep(second, first, 2 * at + 2)
        return carry

    fill_ends(first, tiles)
    lax.fori_loop(0, sweeps // 2, pair, 0)


def core(field, s, tiles):
    return field.at[s, REACH : REACH + tiles]


def fence(plane, planes, halo, total, field):
    for missing, at in ((plane == 0, PAD), (plane == planes - 1, PAD + halo + total)):

        @pl.when(missing)
        def _():
            for t in range(field.shape[0]):
                field[t, at : at + halo] = jnp.full((halo, LANES), far_value, jnp.float32)


def edge_kernel(slabs, p0, p1, p2, p3, even_ref, odd_ref, sem):
    member, plane, _ = here()
    parity = lax.rem(plane, 2)
    sems = Semaphores(sem)
    copies = []
    for j, p in enumerate((p0, p1, p2, p3)):
        first, last = member == j, member == PLANE - 1 - j
        even = ((parity == 0) & last) | ((parity == 1) & first)
        odd = ((parity == 0) & first) | ((parity == 1) & last)
        copies.append((even, sems.copy(p.at[0:slabs], even_ref)))
        copies.append((odd, sems.copy(p.at[0:slabs], odd_ref)))
    run_copies(copies)


def sides(plane, halo, total):
    parity = lax.rem(plane, 2)
    above, below = PAD, PAD + halo + total
    return (
        aligned(parity * above + (1 - parity) * below),
        aligned((1 - parity) * above + parity * below),
    )


def first_kernel(count, halo, planes, edge, has_cost, *refs):
    own, (even, odd), rest = refs[0:4], refs[4:6], refs[6:]
    if has_cost:
        state, low_ref, high_ref, cost_out, one, two, cost, sem = rest
    else:
        cost_in, state, low_ref, high_ref, one, two, cost, sem = rest
    member, plane, _ = here()
    rows = own[0].shape[1]
    total = PLANE * rows
    tiles = cost.shape[1]
    sems = Semaphores(sem)
    even_at, odd_at = sides(plane, halo, total)

    def gather(slabs, field):
        copies = []
        for j in range(PLANE):
            at = aligned(PAD + halo + (member ^ j) * rows)
            copies.append(sems.copy(own[j].at[slabs], field.at[:, pl.ds(at, rows)]))
        for partner, at in ((even, even_at), (odd, odd_at)):
            copies.append(sems.copy(partner.at[slabs], field.at[:, pl.ds(at, halo)]))
        return copies

    copies = []
    for s in range(count):
        copies += gather(slice(s * tiles, (s + 1) * tiles), core(one, s, tiles))
    if has_cost:
        copies += gather(slice(count * tiles, (count + 1) * tiles), cost.at[0])
    else:
        copies.append(sems.copy(cost_in, cost))
    run_copies(copies)
    for s in range(count):
        fence(plane, planes, halo, total, core(one, s, tiles))
    if has_cost:
        fence(plane, planes, halo, total, cost.at[0])
        scale_cost(cost)
    run_sweeps(one, two, cost, count, tiles, FIRST, (total + 2 * halo) // 8)
    parity = lax.rem(plane, 2)
    top, bottom = PAD + halo, PAD + halo + total - edge
    low = aligned(parity * top + (1 - parity) * bottom)
    high = aligned((1 - parity) * top + parity * bottom)
    fields = [core(one, s, tiles) for s in range(count)] + ([cost.at[0]] if has_cost else [])
    copies = []
    for k, field in enumerate(fields):
        slabs = slice(k * tiles, (k + 1) * tiles)
        copies.append(sems.copy(field.at[:, pl.ds(low, edge)], low_ref.at[slabs]))
        copies.append(sems.copy(field.at[:, pl.ds(high, edge)], high_ref.at[slabs]))
        copies.append(sems.copy(field.at[:, PAD + halo : PAD + halo + total], state.at[slabs]))
    if has_cost:
        copies.append(sems.copy(cost, cost_out))
    run_copies(copies)


def last_kernel(count, sweeps, is_last, planes, state, even, odd, base, base_even, base_odd, *rest):
    if is_last:
        partial_ref, each_ref, r0, r1, r2, r3, one, two, cost, best, plain, sem = rest
    else:
        each_ref, best, one, two, cost, sem = rest
    member, plane, _ = here()
    total, halo = state.shape[1], even.shape[1]
    rows = total // PLANE
    tiles = cost.shape[1]
    own = tiles - 1
    sems = Semaphores(sem)
    even_at, odd_at = sides(plane, halo, total)

    def gather(slabs, field, middle, from_even, from_odd):
        return [
            sems.copy(middle.at[slabs], field.at[:, PAD + halo : PAD + halo + total]),
            sems.copy(from_even.at[slabs], field.at[:, pl.ds(even_at, halo)]),
            sems.copy(from_odd.at[slabs], field.at[:, pl.ds(odd_at, halo)]),
        ]

    copies = gather(slice(count * tiles, (count + 1) * tiles), cost.at[0], base, base_even, base_odd)
    for s in range(count):
        copies += gather(slice(s * tiles, (s + 1) * tiles), core(one, s, tiles), state, even, odd)
    run_copies(copies)
    for s in range(count):
        fence(plane, planes, halo, total, core(one, s, tiles))
    fence(plane, planes, halo, total, cost.at[0])
    scale_cost(cost)
    run_sweeps(one, two, cost, count, tiles, sweeps, (total + 2 * halo) // 8)

    for t in range(tiles):
        low = None
        for s in range(count):
            each = jnp.minimum(
                one[s, REACH + t, PAD + halo : PAD + halo + total], jnp.float32(clip_value)
            )
            each = each / clip_value
            each_ref[s * tiles + t] = each
            low = each if low is None else jnp.minimum(low, each)
        best[t] = jnp.minimum(low, partial_ref[t]) if is_last else low
    if not is_last:
        return
    lane = lax.broadcasted_iota(jnp.int32, (8, LANES), 1)
    orders = [((lane + (LANES - j)) * inverse(tiles)) & (LANES - 1) for j in range(tiles)]
    chosen = [lax.rem(lane + t * LANES, tiles) for t in range(own)]

    def back(at, carry):
        spot = pl.ds(aligned(at * 8), 8)
        turned = [gather_lanes(best[j, spot], orders[j]) for j in range(tiles)]
        for t in range(own):
            value = turned[0]
            for j in range(1, tiles):
                value = jnp.where(chosen[t] == j, turned[j], value)
            plain[t, spot] = value
        return carry

    lax.fori_loop(0, total // 8, back, 0)
    run_copies(
        [
            sems.copy(plain.at[:, pl.ds(aligned((member ^ j) * rows), rows)], r)
            for j, r in enumerate((r0, r1, r2, r3))
        ]
    )


def gauge_kernel(cap, half, each_a, each_b, m0, m1, m2, m3, placed_ref, meta, sem):
    def exact(left, pick, right):
        value, found = right if left is None else left, None
        for _ in range(3):
            part = value.astype(jnp.bfloat16)
            value = value - part.astype(jnp.float32)
            pair = (pick, part) if left is None else (part, pick)
            term = jnp.dot(*pair, preferred_element_type=jnp.float32)
            found = term if found is None else found + term
        return found

    member, plane, _ = here()
    sems = Semaphores(sem)
    run_copies(
        [
            sems.copy(m.at[m.shape[0] - 1], meta.at[member ^ j])
            for j, m in enumerate((m0, m1, m2, m3))
        ]
    )
    n, sources, slots = placed_ref.shape
    rows = each_a.shape[1] // PLANE
    tiles = each_a.shape[0] // half
    height = tiles * rows
    lane = lax.broadcasted_iota(jnp.int32, (LANES, LANES), 1).astype(jnp.float32)
    place = lax.broadcasted_iota(jnp.int32, (LANES, height), 1).astype(jnp.float32)
    spot = lax.broadcasted_iota(jnp.int32, (LANES, slots), 1).astype(jnp.float32)
    device = lax.broadcasted_iota(jnp.int32, (n, LANES), 0).astype(jnp.float32)
    filler = jnp.zeros((LANES - meta.shape[1], LANES), jnp.float32)
    offset = (member * height).astype(jnp.float32)
    placed_ref[...] = jnp.zeros(placed_ref.shape, jnp.float32)

    def block_of(q, carry):
        turned = jnp.transpose(jnp.concatenate([meta[q], filler], axis=0))
        pick = jnp.where(turned[:, 0:1] - offset == place, 1.0, 0.0).astype(jnp.bfloat16)
        at_lane = turned[:, 1:2] == lane
        base = ((plane * PLANE + q) * cap).astype(jnp.float32)
        at_slot = turned[:, 3:4] + base == spot
        at_slot = jnp.where(at_slot, 1.0, 0.0).astype(jnp.bfloat16)
        blocks = []
        for s in range(sources):
            each, k = (each_a, s) if s < half else (each_b, s - half)
            block = each[k * tiles : (k + 1) * tiles, pl.ds(aligned(q * rows), rows)]
            blocks.append(block.reshape(height, LANES))
        found = exact(None, pick, jnp.concatenate(blocks, axis=1))
        values = jnp.zeros((LANES, LANES), jnp.float32)
        for s in range(sources):
            mine = jnp.where(at_lane, found[:, s * LANES : (s + 1) * LANES], 0.0)
            values = jnp.where(lane == s, jnp.sum(mine, axis=1, keepdims=True), values)
        values = jnp.transpose(values)
        to_owner = meta[q, 2:3] == device
        sent = [jnp.where(to_owner, values[s : s + 1], 0.0) for s in range(sources)]
        added = exact(jnp.concatenate(sent, axis=0), at_slot, None)
        for s in range(sources):
            placed_ref[:, s] = placed_ref[:, s] + added[s * n : (s + 1) * n]
        return carry

    lax.fori_loop(0, PLANE, block_of, 0)


def join_kernel(r0, r1, r2, r3, gauge_ref, out_ref, result_ref):
    member, _, _ = here()
    tiles, _, _ = r0.shape
    for j, r in enumerate((r0, r1, r2, r3)):
        base = (member ^ j) * (tiles * LANES)
        for t in range(tiles):
            out_ref[:, pl.ds(pl.multiple_of(base + t * LANES, LANES), LANES)] = r[t]
    result_ref[0] = jnp.sum(gauge_ref[...], axis=0)


def shape_of(*dims):
    return jax.ShapeDtypeStruct(dims, jnp.float32)


def on_device(slowness, ocean, start_times, source_cells, gauge_cells, gauge_owner):
    axis = "space"
    n = lax.axis_size(axis)
    rows, width = slowness.shape
    sources = start_times.shape[0]
    gauges = gauge_cells.shape[0]
    planes = n // PLANE
    later_sweeps = SWEEPS * BLOCKS - FIRST
    halo, edge = 2 * FIRST, 2 * later_sweeps
    total = rows * PLANE
    tiles = width // PLANE // LANES + 1
    assert n % (2 * PLANE) == 0 and width % (PLANE * LANES) == 0 and tiles % 2 == 1
    assert gauges == LANES and sources % 2 == 0 and rows == halo
    assert 2 * SWEEPS * BLOCKS <= SIDE and edge <= total and FIRST % 2 == later_sweeps % 2 == 0
    assert total % 16 == halo % 8 == edge % 8 == 0
    cap = max(2, 2 * gauges // n)
    half = sources // 2
    groups = (tuple(range(half)), tuple(range(half, sources)))
    size = half * tiles
    sizes = [size + tiles + 1, size]

    def call(kernel, out_shape, in_specs, out_specs, scratch, micros=2):
        return pl.pallas_call(
            kernel,
            out_shape=out_shape,
            in_specs=in_specs,
            out_specs=out_specs,
            scratch_shapes=scratch,
            compiler_params=pltpu.CompilerParams(vmem_limit_bytes=VMEM_BYTES),
            cost_estimate=pl.CostEstimate(
                flops=0, bytes_accessed=3_000_000 * micros, transcendentals=0
            ),
        )

    def vmem(*dims):
        return pltpu.VMEM(dims, jnp.float32)

    def semaphores(number):
        return pltpu.SemaphoreType.DMA((number,))

    def pack(k):
        fields = half + (k == 0)
        more = [slowness, ocean, gauge_cells.reshape(1, gauges), gauge_owner.reshape(1, gauges)]
        inputs = [source_cells, start_times] + (more if k == 0 else [])
        line = pltpu.VMEM((1, gauges), jnp.int32)
        return call(
            functools.partial(pack_kernel, groups[k], k == 0),
            [shape_of(sizes[k], rows, LANES)] * PLANE,
            [HBM] * len(inputs),
            [VMEM] * PLANE,
            [pltpu.SMEM((sources,), jnp.int32)]
            + ([line, line] if k == 0 else [])
            + [vmem(fields, rows, width)]
            + ([pltpu.VMEM((rows, width), jnp.int32)] if k == 0 else [])
            + [vmem(PLANE, fields, rows, LANES), semaphores(6)],
        )(*(pltpu.with_memory_space_constraint(x, pltpu.HBM) for x in inputs))

    def swap(x, j):
        return lax.ppermute(x, axis, [(d, d ^ j) for d in range(n)])

    def swap_planes(even, odd):
        pairs_even = [(d, (d // PLANE ^ 1) * PLANE + d % PLANE) for d in range(n)]
        pairs_odd = [
            (d, (((d // PLANE + 1) ^ 1) - 1) * PLANE + d % PLANE)
            for d in range(PLANE, n - PLANE)
        ]
        return lax.ppermute(even, axis, pairs_even), lax.ppermute(odd, axis, pairs_odd)

    pieces, beside = [], []
    for k in range(2):
        mine = pack(k)
        pieces.append([mine[0]] + [swap(mine[j], j) for j in range(1, PLANE)])
    for k in range(2):
        slabs = size + (tiles if k == 0 else 0)
        edge_call = call(
            functools.partial(edge_kernel, slabs),
            [shape_of(slabs, rows, LANES)] * 2,
            [ANY] * PLANE,
            [ANY] * 2,
            [semaphores(2 * PLANE)],
            1,
        )
        edges = edge_call(*pieces[k])
        beside.append(swap_planes(*edges))

    def buffers(deep):
        deep += 3 * PAD
        ends = tiles + 2 * REACH
        return [vmem(half, ends, deep, LANES), vmem(half, ends, deep, LANES), vmem(3, tiles, deep, LANES)]

    states, later, cost = [], [], None
    for k in range(2):
        slabs = size + (tiles if k == 0 else 0)
        scratch = buffers(total + 2 * halo)
        outs = call(
            functools.partial(first_kernel, half, halo, planes, edge, k == 0),
            [shape_of(slabs, total, LANES)]
            + [shape_of(slabs, edge, LANES)] * 2
            + ([shape_of(*scratch[2].shape)] if k == 0 else []),
            [ANY] * (PLANE + 2 + k),
            [ANY] * (4 - k),
            scratch + [semaphores((PLANE + 2) * (half + 1) + 3 * half + 4)],
            7,
        )(*pieces[k], *beside[k], *([] if k == 0 else [cost]))
        if k == 0:
            cost = outs[3]
        states.append(outs[0])
        later.append(swap_planes(outs[1], outs[2]))

    slots = n * cap
    each, partial = [], None
    for k in range(2):
        out_shape, out_specs, more = [shape_of(size, total, LANES)], [VMEM], []
        if k == 0:
            out_shape.append(shape_of(tiles, total, LANES))
            out_specs.append(VMEM)
        else:
            out_shape += [shape_of(tiles - 1, rows, LANES)] * PLANE
            out_specs += [ANY] * PLANE
            more = [vmem(tiles, total, LANES), vmem(tiles - 1, total, LANES)]
        outs = call(
            functools.partial(last_kernel, half, later_sweeps, k == 1, planes),
            out_shape,
            [ANY] * 6 + [VMEM] * k,
            out_specs,
            buffers(total + 2 * edge) + more + [semaphores(3 * (half + 1) + PLANE)],
            15,
        )(states[k], *later[k], states[0], *later[0], *([] if k == 0 else [partial]))
        each.append(outs[0])
        if k == 0:
            partial = outs[1]
        else:
            returned = outs[1:]

    back = [returned[0]] + [swap(returned[j], j) for j in range(1, PLANE)]
    gauge_call = call(
        functools.partial(gauge_kernel, cap, half),
        shape_of(n, sources, slots),
        [VMEM] * 2 + [ANY] * PLANE,
        VMEM,
        [vmem(PLANE, rows, LANES), semaphores(PLANE)],
        4,
    )
    placed = gauge_call(*each, *pieces[0])
    received = lax.all_to_all(placed, axis, split_axis=0, concat_axis=0, tiled=True)
    return call(
        join_kernel,
        (shape_of(rows, width), shape_of(1, sources, slots)),
        [VMEM] * (PLANE + 1),
        (VMEM, VMEM),
        [],
    )(*back, received)


def solution(mesh):
    return jax.shard_map(
        on_device,
        mesh=mesh,
        in_specs=(
            P(("groups", "space"), None),
            P(("groups", "space"), None),
            P("groups", "space", None),
            P("groups"),
            P(("groups", "space")),
            P(("groups", "space"), None),
        ),
        out_specs=(P(("groups", "space"), None), P(("groups", "space"), None, None)),
        check_vma=False,
    )
```

```python
import functools
import jax
import jax.numpy as jnp
from jax import lax
from jax.experimental import pallas as pl
from jax.experimental.pallas import tpu as pltpu
from jax.sharding import PartitionSpec as P

SWEEPS = 8
BLOCKS = 3
FIRST = 8

far_value = 1000000.0
land_cost = 10000.0
clip_value = 48.0
root_two = 1.41421356
root_five = 2.23606798

PLANE = 4
LANES = 128
SIDE = 64
PAD = 8
REACH = 2
VMEM_BYTES = 24 * 1024 * 1024
ANY = pl.BlockSpec(memory_space=pl.ANY)
HBM = pl.BlockSpec(memory_space=pltpu.HBM)
SMEM = pl.BlockSpec(memory_space=pltpu.SMEM)
VMEM = pl.BlockSpec(memory_space=pltpu.VMEM)


def run_copies(copies):
    def each(act):
        for copy in copies:
            if isinstance(copy, tuple):
                pl.when(copy[0])(functools.partial(act, copy[1]))
            else:
                act(copy)

    each(lambda copy: copy.start())
    each(lambda copy: copy.wait())


class Semaphores:
    def __init__(self, sem):
        self.sem, self.used = sem, 0

    def copy(self, source, target):
        self.used += 1
        return pltpu.make_async_copy(source, target, self.sem.at[self.used - 1])


def inverse(number):
    return pow(number, -1, LANES)


def gather_lanes(x, order):
    return jnp.take_along_axis(x, order, axis=1, mode="promise_in_bounds")


def here():
    index = lax.axis_index("space")
    return lax.rem(index, PLANE), lax.div(index, PLANE), index


def aligned(at):
    return pl.multiple_of(at, 8)


def pack_kernel(group, has_cost, source_hbm, start_hbm, *rest):
    if has_cost:
        slow_hbm, ocean_hbm, cell_hbm, owner_hbm, *outs = rest[:-7]
        source_ref, cell_ref, owner_ref, field_ref, ocean_ref, side_ref, sem = rest[-7:]
    else:
        outs = rest[:-4]
        source_ref, field_ref, side_ref, sem = rest[-4:]
    _, rows, width = start_hbm.shape
    sources = len(group)
    fields = field_ref.shape[0]
    own = width // PLANE
    tiles = own // LANES
    chunk = tiles + 1
    member, _, index = here()
    sems = Semaphores(sem)
    copies = [
        sems.copy(start_hbm.at[group[0] : group[-1] + 1], field_ref.at[0:sources]),
        sems.copy(source_hbm, source_ref),
    ]
    if has_cost:
        copies += [
            sems.copy(slow_hbm, field_ref.at[sources]),
            sems.copy(ocean_hbm, ocean_ref),
            sems.copy(cell_hbm, cell_ref),
            sems.copy(owner_hbm, owner_ref),
        ]
    run_copies(copies)
    lane = lax.broadcasted_iota(jnp.int32, (8, LANES), 1)
    row = lax.broadcasted_iota(jnp.int32, (8, LANES), 0)
    far = jnp.full((8, LANES), far_value, jnp.float32)

    for t in range(width // LANES if has_cost else 0):
        at = slice(t * LANES, (t + 1) * LANES)
        field_ref[sources, :, at] = jnp.where(
            ocean_ref[:, at] == 1, field_ref[sources, :, at], jnp.float32(land_cost)
        )
    for s in range(sources):
        cell = source_ref[group[s]] - index * (rows * width)

        @pl.when((cell >= 0) & (cell < rows * width))
        def _():
            line, column = lax.div(cell, width), lax.rem(cell, width)
            spot = pl.ds(aligned(lax.div(line, 8) * 8), 8)
            at = pl.ds(pl.multiple_of(lax.div(column, LANES) * LANES, LANES), LANES)
            hit = (row == lax.rem(line, 8)) & (lane == lax.rem(column, LANES))
            field_ref[s, spot, at] = jnp.where(hit, 0.0, field_ref[s, spot, at])

    for f in range(fields):
        for w in range(PLANE):
            for half in range(0, rows, 8):
                right = (w + 1) * own
                left = w * own - LANES
                value_right = field_ref[f, half : half + 8, right : right + LANES] if w < PLANE - 1 else far
                value_left = field_ref[f, half : half + 8, left : left + LANES] if w > 0 else far
                side_ref[w, f, half : half + 8] = jnp.where(lane < SIDE, value_right, value_left)

    def convert(j, carry):
        column = (((lane + (LANES - j)) * inverse(chunk)) & (LANES - 1)) * chunk + j
        masks = [column >= t * LANES for t in range(1, chunk)]
        order = (lane * chunk + j) & (LANES - 1)
        for shift in range(PLANE):
            window = member ^ shift
            out = outs[shift]
            for f in range(fields):
                for half in range(0, rows, 8):
                    mixed = None
                    for t in range(chunk):
                        if t < tiles:
                            at = pl.multiple_of(window * own + t * LANES, LANES)
                            value = field_ref[f, half : half + 8, pl.ds(at, LANES)]
                        else:
                            value = side_ref[window, f, half : half + 8]
                        mixed = value if t == 0 else jnp.where(masks[t - 1], value, mixed)
                    out[f * chunk + j, half : half + 8] = gather_lanes(mixed, order)
        return carry

    lax.fori_loop(0, chunk, convert, 0)
    if not has_cost:
        return

    owner = owner_ref[...].astype(jnp.float32)
    across = jnp.broadcast_to(owner, (LANES, LANES))
    down = jnp.transpose(across)
    earlier = lax.broadcasted_iota(jnp.int32, (LANES, LANES), 0) < lax.broadcasted_iota(
        jnp.int32, (LANES, LANES), 1
    )
    rank = jnp.sum(jnp.where(earlier & (across == down), 1.0, 0.0), axis=0, keepdims=True)
    cell = cell_ref[...].astype(jnp.float32)
    line = jnp.floor(cell / width)
    column = cell - line * width
    part = jnp.floor(column / own)
    column = column - part * own
    spot = jnp.floor((column + 0.5) / chunk)
    place = (part * chunk + (column - spot * chunk)) * rows + line
    filler = jnp.zeros((rows - 4, LANES), jnp.float32)
    meta = jnp.concatenate([place, spot, owner, rank, filler], axis=0)
    for shift in range(PLANE):
        outs[shift][outs[shift].shape[0] - 1] = meta


def keep_ends(dst, s, t, spot, value, tiles):
    if t < REACH:
        dst[s, tiles + REACH + t, spot] = pltpu.roll(value, LANES - 1, 1)
    if t >= tiles - REACH:
        dst[s, t - (tiles - REACH), spot] = pltpu.roll(value, 1, 1)


def relax_rows(src, dst, cost, count, tiles, start):
    spot = pl.ds(start, 8)
    order = sorted(range(tiles), key=lambda t: REACH <= t < tiles - REACH)
    for s in range(count):

        def load(t, shift):
            return src[s, t + REACH, pl.ds(start + shift, 8)]

        near = {t: load(t, 0) for t in range(-1, tiles + 1)}
        one = {t: jnp.minimum(load(t, -1), load(t, 1)) for t in range(-2, tiles + 2)}
        two = {t: jnp.minimum(load(t, -2), load(t, 2)) for t in range(-1, tiles + 1)}
        for t in order:
            m1 = jnp.minimum(one[t], jnp.minimum(near[t - 1], near[t + 1]))
            m2 = jnp.minimum(one[t - 1], one[t + 1])
            m5 = jnp.minimum(
                jnp.minimum(one[t - 2], one[t + 2]), jnp.minimum(two[t - 1], two[t + 1])
            )
            best = jnp.minimum(m1 + cost[0, t, spot], m2 + cost[1, t, spot])
            best = jnp.minimum(best, m5 + cost[2, t, spot])
            value = jnp.minimum(near[t], best)
            dst[s, t + REACH, spot] = value


def fill_rows(field, tiles, start):
    spot = pl.ds(start, 8)
    for s in range(field.shape[0]):
        for t in list(range(REACH)) + list(range(tiles - REACH, tiles)):
            keep_ends(field, s, t, spot, field[s, t + REACH, spot], tiles)


def fill_ends(field, tiles):
    def group(at, carry):
        for k in range(2):
            fill_rows(field, tiles, pl.multiple_of(PAD + at * 16 + k * 8, 8))
        return carry

    lax.fori_loop(0, (field.shape[2] - 3 * PAD) // 16, group, 0)


def scale_cost(cost):
    def group(at, carry):
        spot = pl.ds(pl.multiple_of(at * 8, 8), 8)
        for t in range(cost.shape[1]):
            value = cost[0, t, spot]
            cost[1, t, spot] = root_two * value
            cost[2, t, spot] = root_five * value
        return carry

    lax.fori_loop(0, cost.shape[2] // 8, group, 0)


def run_sweeps(first, second, cost, count, tiles, sweeps, groups):
    def sweep(src, dst, number):
        low = lax.shift_right_logical(number, 2)

        for step in range(sweeps // 4 + 1):

            @pl.when(low == step)
            def _():
                for at in range(step, groups - step):
                    fill_rows(dst, tiles, PAD + 8 * at - 8)
                    relax_rows(src, dst, cost, count, tiles, PAD + 8 * at)
                fill_rows(dst, tiles, PAD + 8 * (groups - step - 1))

    def pair(at, carry):
        sweep(first, second, 2 * at + 1)
        sweep(second, first, 2 * at + 2)
        return carry

    fill_ends(first, tiles)
    lax.fori_loop(0, sweeps // 2, pair, 0)


def core(field, s, tiles):
    return field.at[s, REACH : REACH + tiles]


def fence(plane, planes, halo, total, field):
    for missing, at in ((plane == 0, PAD), (plane == planes - 1, PAD + halo + total)):

        @pl.when(missing)
        def _():
            for t in range(field.shape[0]):
                field[t, at : at + halo] = jnp.full((halo, LANES), far_value, jnp.float32)


def edge_kernel(slabs, p0, p1, p2, p3, even_ref, odd_ref, sem):
    member, plane, _ = here()
    parity = lax.rem(plane, 2)
    sems = Semaphores(sem)
    copies = []
    for j, p in enumerate((p0, p1, p2, p3)):
        first, last = member == j, member == PLANE - 1 - j
        even = ((parity == 0) & last) | ((parity == 1) & first)
        odd = ((parity == 0) & first) | ((parity == 1) & last)
        copies.append((even, sems.copy(p.at[0:slabs], even_ref)))
        copies.append((odd, sems.copy(p.at[0:slabs], odd_ref)))
    run_copies(copies)


def sides(plane, halo, total):
    parity = lax.rem(plane, 2)
    above, below = PAD, PAD + halo + total
    return (
        aligned(parity * above + (1 - parity) * below),
        aligned((1 - parity) * above + parity * below),
    )


def first_kernel(count, halo, planes, edge, has_cost, *refs):
    own, (even, odd), rest = refs[0:4], refs[4:6], refs[6:]
    if has_cost:
        state, low_ref, high_ref, cost_out, one, two, cost, sem = rest
    else:
        cost_in, state, low_ref, high_ref, one, two, cost, sem = rest
    member, plane, _ = here()
    rows = own[0].shape[1]
    total = PLANE * rows
    tiles = cost.shape[1]
    sems = Semaphores(sem)
    even_at, odd_at = sides(plane, halo, total)

    def gather(slabs, field):
        copies = []
        for j in range(PLANE):
            at = aligned(PAD + halo + (member ^ j) * rows)
            copies.append(sems.copy(own[j].at[slabs], field.at[:, pl.ds(at, rows)]))
        for partner, at in ((even, even_at), (odd, odd_at)):
            copies.append(sems.copy(partner.at[slabs], field.at[:, pl.ds(at, halo)]))
        return copies

    copies = []
    for s in range(count):
        copies += gather(slice(s * tiles, (s + 1) * tiles), core(one, s, tiles))
    if has_cost:
        copies += gather(slice(count * tiles, (count + 1) * tiles), cost.at[0])
    else:
        copies.append(sems.copy(cost_in, cost))
    run_copies(copies)
    for s in range(count):
        fence(plane, planes, halo, total, core(one, s, tiles))
    if has_cost:
        fence(plane, planes, halo, total, cost.at[0])
        scale_cost(cost)
    run_sweeps(one, two, cost, count, tiles, FIRST, (total + 2 * halo) // 8)
    parity = lax.rem(plane, 2)
    top, bottom = PAD + halo, PAD + halo + total - edge
    low = aligned(parity * top + (1 - parity) * bottom)
    high = aligned((1 - parity) * top + parity * bottom)
    fields = [core(one, s, tiles) for s in range(count)] + ([cost.at[0]] if has_cost else [])
    copies = []
    for k, field in enumerate(fields):
        slabs = slice(k * tiles, (k + 1) * tiles)
        copies.append(sems.copy(field.at[:, pl.ds(low, edge)], low_ref.at[slabs]))
        copies.append(sems.copy(field.at[:, pl.ds(high, edge)], high_ref.at[slabs]))
        copies.append(sems.copy(field.at[:, PAD + halo : PAD + halo + total], state.at[slabs]))
    if has_cost:
        copies.append(sems.copy(cost, cost_out))
    run_copies(copies)


def last_kernel(count, sweeps, is_last, planes, state, even, odd, base, base_even, base_odd, *rest):
    if is_last:
        partial_ref, each_ref, r0, r1, r2, r3, one, two, cost, best, plain, sem = rest
    else:
        each_ref, best, one, two, cost, sem = rest
    member, plane, _ = here()
    total, halo = state.shape[1], even.shape[1]
    rows = total // PLANE
    tiles = cost.shape[1]
    own = tiles - 1
    sems = Semaphores(sem)
    even_at, odd_at = sides(plane, halo, total)

    def gather(slabs, field, middle, from_even, from_odd):
        return [
            sems.copy(middle.at[slabs], field.at[:, PAD + halo : PAD + halo + total]),
            sems.copy(from_even.at[slabs], field.at[:, pl.ds(even_at, halo)]),
            sems.copy(from_odd.at[slabs], field.at[:, pl.ds(odd_at, halo)]),
        ]

    copies = gather(slice(count * tiles, (count + 1) * tiles), cost.at[0], base, base_even, base_odd)
    for s in range(count):
        copies += gather(slice(s * tiles, (s + 1) * tiles), core(one, s, tiles), state, even, odd)
    run_copies(copies)
    for s in range(count):
        fence(plane, planes, halo, total, core(one, s, tiles))
    fence(plane, planes, halo, total, cost.at[0])
    scale_cost(cost)
    run_sweeps(one, two, cost, count, tiles, sweeps, (total + 2 * halo) // 8)

    for t in range(tiles):
        low = None
        for s in range(count):
            each = jnp.minimum(
                one[s, REACH + t, PAD + halo : PAD + halo + total], jnp.float32(clip_value)
            )
            each = each / clip_value
            each_ref[s * tiles + t] = each
            low = each if low is None else jnp.minimum(low, each)
        best[t] = jnp.minimum(low, partial_ref[t]) if is_last else low
    if not is_last:
        return
    lane = lax.broadcasted_iota(jnp.int32, (8, LANES), 1)
    orders = [((lane + (LANES - j)) * inverse(tiles)) & (LANES - 1) for j in range(tiles)]
    chosen = [lax.rem(lane + t * LANES, tiles) for t in range(own)]

    def back(at, carry):
        spot = pl.ds(aligned(at * 8), 8)
        turned = [gather_lanes(best[j, spot], orders[j]) for j in range(tiles)]
        for t in range(own):
            value = turned[0]
            for j in range(1, tiles):
                value = jnp.where(chosen[t] == j, turned[j], value)
            plain[t, spot] = value
        return carry

    lax.fori_loop(0, total // 8, back, 0)
    run_copies(
        [
            sems.copy(plain.at[:, pl.ds(aligned((member ^ j) * rows), rows)], r)
            for j, r in enumerate((r0, r1, r2, r3))
        ]
    )


def gauge_kernel(cap, half, each_a, each_b, m0, m1, m2, m3, placed_ref, meta, sem):
    def exact(left, pick, right):
        value, found = right if left is None else left, None
        for _ in range(3):
            part = value.astype(jnp.bfloat16)
            value = value - part.astype(jnp.float32)
            pair = (pick, part) if left is None else (part, pick)
            term = jnp.dot(*pair, preferred_element_type=jnp.float32)
            found = term if found is None else found + term
        return found

    member, plane, _ = here()
    sems = Semaphores(sem)
    run_copies(
        [
            sems.copy(m.at[m.shape[0] - 1], meta.at[member ^ j])
            for j, m in enumerate((m0, m1, m2, m3))
        ]
    )
    n, sources, slots = placed_ref.shape
    rows = each_a.shape[1] // PLANE
    tiles = each_a.shape[0] // half
    height = tiles * rows
    lane = lax.broadcasted_iota(jnp.int32, (LANES, LANES), 1).astype(jnp.float32)
    place = lax.broadcasted_iota(jnp.int32, (LANES, height), 1).astype(jnp.float32)
    spot = lax.broadcasted_iota(jnp.int32, (LANES, slots), 1).astype(jnp.float32)
    device = lax.broadcasted_iota(jnp.int32, (n, LANES), 0).astype(jnp.float32)
    filler = jnp.zeros((LANES - meta.shape[1], LANES), jnp.float32)
    offset = (member * height).astype(jnp.float32)
    totals = [None] * sources
    for q in range(PLANE):
        turned = jnp.transpose(jnp.concatenate([meta[q], filler], axis=0))
        pick = jnp.where(turned[:, 0:1] - offset == place, 1.0, 0.0).astype(jnp.bfloat16)
        at_lane = turned[:, 1:2] == lane
        base = ((plane * PLANE + q) * cap).astype(jnp.float32)
        at_slot = turned[:, 3:4] + base == spot
        at_slot = jnp.where(at_slot, 1.0, 0.0).astype(jnp.bfloat16)
        blocks = []
        for s in range(sources):
            each, k = (each_a, s) if s < half else (each_b, s - half)
            block = each[k * tiles : (k + 1) * tiles, q * rows : (q + 1) * rows]
            blocks.append(block.reshape(height, LANES))
        found = exact(None, pick, jnp.concatenate(blocks, axis=1))
        values = jnp.zeros((LANES, LANES), jnp.float32)
        for s in range(sources):
            mine = jnp.where(at_lane, found[:, s * LANES : (s + 1) * LANES], 0.0)
            values = jnp.where(lane == s, jnp.sum(mine, axis=1, keepdims=True), values)
        values = jnp.transpose(values)
        to_owner = meta[q, 2:3] == device
        sent = [jnp.where(to_owner, values[s : s + 1], 0.0) for s in range(sources)]
        added = exact(jnp.concatenate(sent, axis=0), at_slot, None)
        for s in range(sources):
            term = added[s * n : (s + 1) * n]
            totals[s] = term if q == 0 else totals[s] + term
    for s in range(sources):
        placed_ref[:, s] = totals[s]


def join_kernel(r0, r1, r2, r3, gauge_ref, out_ref, result_ref):
    member, _, _ = here()
    tiles, _, _ = r0.shape
    for j, r in enumerate((r0, r1, r2, r3)):
        base = (member ^ j) * (tiles * LANES)
        for t in range(tiles):
            out_ref[:, pl.ds(pl.multiple_of(base + t * LANES, LANES), LANES)] = r[t]
    result_ref[0] = jnp.sum(gauge_ref[...], axis=0)


def shape_of(*dims):
    return jax.ShapeDtypeStruct(dims, jnp.float32)


def on_device(slowness, ocean, start_times, source_cells, gauge_cells, gauge_owner):
    axis = "space"
    n = lax.axis_size(axis)
    rows, width = slowness.shape
    sources = start_times.shape[0]
    gauges = gauge_cells.shape[0]
    planes = n // PLANE
    later_sweeps = SWEEPS * BLOCKS - FIRST
    halo, edge = 2 * FIRST, 2 * later_sweeps
    total = rows * PLANE
    tiles = width // PLANE // LANES + 1
    assert n % (2 * PLANE) == 0 and width % (PLANE * LANES) == 0 and tiles % 2 == 1
    assert gauges == LANES and sources % 2 == 0 and rows == halo
    assert 2 * SWEEPS * BLOCKS <= SIDE and edge <= total and FIRST % 2 == later_sweeps % 2 == 0
    assert total % 16 == halo % 8 == edge % 8 == 0
    cap = max(2, 2 * gauges // n)
    half = sources // 2
    groups = (tuple(range(half)), tuple(range(half, sources)))
    size = half * tiles
    sizes = [size + tiles + 1, size]

    def call(kernel, out_shape, in_specs, out_specs, scratch, micros=2):
        return pl.pallas_call(
            kernel,
            out_shape=out_shape,
            in_specs=in_specs,
            out_specs=out_specs,
            scratch_shapes=scratch,
            compiler_params=pltpu.CompilerParams(vmem_limit_bytes=VMEM_BYTES),
            cost_estimate=pl.CostEstimate(
                flops=0, bytes_accessed=3_000_000 * micros, transcendentals=0
            ),
        )

    def vmem(*dims):
        return pltpu.VMEM(dims, jnp.float32)

    def semaphores(number):
        return pltpu.SemaphoreType.DMA((number,))

    def pack(k):
        fields = half + (k == 0)
        more = [slowness, ocean, gauge_cells.reshape(1, gauges), gauge_owner.reshape(1, gauges)]
        inputs = [source_cells, start_times] + (more if k == 0 else [])
        line = pltpu.VMEM((1, gauges), jnp.int32)
        return call(
            functools.partial(pack_kernel, groups[k], k == 0),
            [shape_of(sizes[k], rows, LANES)] * PLANE,
            [HBM] * len(inputs),
            [VMEM] * PLANE,
            [pltpu.SMEM((sources,), jnp.int32)]
            + ([line, line] if k == 0 else [])
            + [vmem(fields, rows, width)]
            + ([pltpu.VMEM((rows, width), jnp.int32)] if k == 0 else [])
            + [vmem(PLANE, fields, rows, LANES), semaphores(6)],
        )(*(pltpu.with_memory_space_constraint(x, pltpu.HBM) for x in inputs))

    def swap(x, j):
        return lax.ppermute(x, axis, [(d, d ^ j) for d in range(n)])

    def swap_planes(even, odd):
        pairs_even = [(d, (d // PLANE ^ 1) * PLANE + d % PLANE) for d in range(n)]
        pairs_odd = [
            (d, (((d // PLANE + 1) ^ 1) - 1) * PLANE + d % PLANE)
            for d in range(PLANE, n - PLANE)
        ]
        return lax.ppermute(even, axis, pairs_even), lax.ppermute(odd, axis, pairs_odd)

    pieces, beside = [], []
    for k in range(2):
        mine = pack(k)
        pieces.append([mine[0]] + [swap(mine[j], j) for j in range(1, PLANE)])
    for k in range(2):
        slabs = size + (tiles if k == 0 else 0)
        edge_call = call(
            functools.partial(edge_kernel, slabs),
            [shape_of(slabs, rows, LANES)] * 2,
            [ANY] * PLANE,
            [ANY] * 2,
            [semaphores(2 * PLANE)],
            1,
        )
        edges = edge_call(*pieces[k])
        beside.append(swap_planes(*edges))

    def buffers(deep):
        deep += 3 * PAD
        ends = tiles + 2 * REACH
        return [vmem(half, ends, deep, LANES), vmem(half, ends, deep, LANES), vmem(3, tiles, deep, LANES)]

    states, later, cost = [], [], None
    for k in range(2):
        slabs = size + (tiles if k == 0 else 0)
        scratch = buffers(total + 2 * halo)
        first_call = call(
            functools.partial(first_kernel, half, halo, planes, edge, k == 0),
            [shape_of(slabs, total, LANES)]
            + [shape_of(slabs, edge, LANES)] * 2
            + ([shape_of(*scratch[2].shape)] if k == 0 else []),
            [ANY] * (PLANE + 2 + k),
            [ANY] * (4 - k),
            scratch + [semaphores((PLANE + 2) * (half + 1) + 3 * half + 4)],
            7,
        )
        outs = first_call(*pieces[k], *beside[k], *([] if k == 0 else [cost]))
        if k == 0:
            cost = outs[3]
        states.append(outs[0])
        later.append(swap_planes(outs[1], outs[2]))

    slots = n * cap
    each, partial = [], None
    for k in range(2):
        out_shape, out_specs, more = [shape_of(size, total, LANES)], [VMEM], []
        if k == 0:
            out_shape.append(shape_of(tiles, total, LANES))
            out_specs.append(VMEM)
        else:
            out_shape += [shape_of(tiles - 1, rows, LANES)] * PLANE
            out_specs += [ANY] * PLANE
            more = [vmem(tiles, total, LANES), vmem(tiles - 1, total, LANES)]
        outs = call(
            functools.partial(last_kernel, half, later_sweeps, k == 1, planes),
            out_shape,
            [ANY] * 6 + [VMEM] * k,
            out_specs,
            buffers(total + 2 * edge) + more + [semaphores(3 * (half + 1) + PLANE)],
            15,
        )(states[k], *later[k], states[0], *later[0], *([] if k == 0 else [partial]))
        each.append(outs[0])
        if k == 0:
            partial = outs[1]
        else:
            returned = outs[1:]

    back = [returned[0]] + [swap(returned[j], j) for j in range(1, PLANE)]
    gauge_call = call(
        functools.partial(gauge_kernel, cap, half),
        shape_of(n, sources, slots),
        [VMEM] * 2 + [ANY] * PLANE,
        VMEM,
        [vmem(PLANE, rows, LANES), semaphores(PLANE)],
        4,
    )
    placed = gauge_call(*each, *pieces[0])
    received = lax.all_to_all(placed, axis, split_axis=0, concat_axis=0, tiled=True)
    return call(
        join_kernel,
        (shape_of(rows, width), shape_of(1, sources, slots)),
        [VMEM] * (PLANE + 1),
        (VMEM, VMEM),
        [],
    )(*back, received)


def solution(mesh):
    return jax.shard_map(
        on_device,
        mesh=mesh,
        in_specs=(
            P(("groups", "space"), None),
            P(("groups", "space"), None),
            P("groups", "space", None),
            P("groups"),
            P(("groups", "space")),
            P(("groups", "space"), None),
        ),
        out_specs=(P(("groups", "space"), None), P(("groups", "space"), None, None)),
        check_vma=False,
    )
```

```python
import functools
import jax
import jax.numpy as jnp
from jax import lax
from jax.experimental import pallas as pl
from jax.experimental.pallas import tpu as pltpu
from jax.sharding import PartitionSpec as P

SWEEPS = 8
BLOCKS = 3
FIRST = 8

far_value = 1000000.0
land_cost = 10000.0
clip_value = 48.0
root_two = 1.41421356
root_five = 2.23606798

PLANE = 4
LANES = 128
SIDE = 64
PAD = 8
REACH = 2
VMEM_BYTES = 24 * 1024 * 1024
ANY = pl.BlockSpec(memory_space=pl.ANY)
HBM = pl.BlockSpec(memory_space=pltpu.HBM)
SMEM = pl.BlockSpec(memory_space=pltpu.SMEM)
VMEM = pl.BlockSpec(memory_space=pltpu.VMEM)


def run_copies(copies):
    def each(act):
        for copy in copies:
            if isinstance(copy, tuple):
                pl.when(copy[0])(functools.partial(act, copy[1]))
            else:
                act(copy)

    each(lambda copy: copy.start())
    each(lambda copy: copy.wait())


class Semaphores:
    def __init__(self, sem):
        self.sem, self.used = sem, 0

    def copy(self, source, target):
        self.used += 1
        return pltpu.make_async_copy(source, target, self.sem.at[self.used - 1])


def inverse(number):
    return pow(number, -1, LANES)


def gather_lanes(x, order):
    return jnp.take_along_axis(x, order, axis=1, mode="promise_in_bounds")


def here():
    index = lax.axis_index("space")
    return lax.rem(index, PLANE), lax.div(index, PLANE), index


def aligned(at):
    return pl.multiple_of(at, 8)


def pack_kernel(group, has_cost, source_hbm, start_hbm, *rest):
    if has_cost:
        slow_hbm, ocean_hbm, cell_hbm, owner_hbm, *outs = rest[:-7]
        source_ref, cell_ref, owner_ref, field_ref, ocean_ref, side_ref, sem = rest[-7:]
    else:
        outs = rest[:-4]
        source_ref, field_ref, side_ref, sem = rest[-4:]
    _, rows, width = start_hbm.shape
    sources = len(group)
    fields = field_ref.shape[0]
    own = width // PLANE
    tiles = own // LANES
    chunk = tiles + 1
    member, _, index = here()
    sems = Semaphores(sem)
    copies = [
        sems.copy(start_hbm.at[group[0] : group[-1] + 1], field_ref.at[0:sources]),
        sems.copy(source_hbm, source_ref),
    ]
    if has_cost:
        copies += [
            sems.copy(slow_hbm, field_ref.at[sources]),
            sems.copy(ocean_hbm, ocean_ref),
            sems.copy(cell_hbm, cell_ref),
            sems.copy(owner_hbm, owner_ref),
        ]
    run_copies(copies)
    lane = lax.broadcasted_iota(jnp.int32, (8, LANES), 1)
    row = lax.broadcasted_iota(jnp.int32, (8, LANES), 0)
    far = jnp.full((8, LANES), far_value, jnp.float32)

    for t in range(width // LANES if has_cost else 0):
        at = slice(t * LANES, (t + 1) * LANES)
        field_ref[sources, :, at] = jnp.where(
            ocean_ref[:, at] == 1, field_ref[sources, :, at], jnp.float32(land_cost)
        )
    for s in range(sources):
        cell = source_ref[group[s]] - index * (rows * width)

        @pl.when((cell >= 0) & (cell < rows * width))
        def _():
            line, column = lax.div(cell, width), lax.rem(cell, width)
            spot = pl.ds(aligned(lax.div(line, 8) * 8), 8)
            at = pl.ds(pl.multiple_of(lax.div(column, LANES) * LANES, LANES), LANES)
            hit = (row == lax.rem(line, 8)) & (lane == lax.rem(column, LANES))
            field_ref[s, spot, at] = jnp.where(hit, 0.0, field_ref[s, spot, at])

    for f in range(fields):
        for w in range(PLANE):
            for half in range(0, rows, 8):
                right = (w + 1) * own
                left = w * own - LANES
                value_right = field_ref[f, half : half + 8, right : right + LANES] if w < PLANE - 1 else far
                value_left = field_ref[f, half : half + 8, left : left + LANES] if w > 0 else far
                side_ref[w, f, half : half + 8] = jnp.where(lane < SIDE, value_right, value_left)

    for j in range(chunk):
        column = (((lane + (LANES - j)) * inverse(chunk)) & (LANES - 1)) * chunk + j
        masks = [column >= t * LANES for t in range(1, chunk)]
        order = (lane * chunk + j) & (LANES - 1)
        for shift in range(PLANE):
            window = member ^ shift
            out = outs[shift]
            for f in range(fields):
                for half in range(0, rows, 8):
                    mixed = None
                    for t in range(chunk):
                        if t < tiles:
                            at = pl.multiple_of(window * own + t * LANES, LANES)
                            value = field_ref[f, half : half + 8, pl.ds(at, LANES)]
                        else:
                            value = side_ref[window, f, half : half + 8]
                        mixed = value if t == 0 else jnp.where(masks[t - 1], value, mixed)
                    out[f * chunk + j, half : half + 8] = gather_lanes(mixed, order)
    if not has_cost:
        return

    owner = owner_ref[...].astype(jnp.float32)
    across = jnp.broadcast_to(owner, (LANES, LANES))
    down = jnp.transpose(across)
    earlier = lax.broadcasted_iota(jnp.int32, (LANES, LANES), 0) < lax.broadcasted_iota(
        jnp.int32, (LANES, LANES), 1
    )
    rank = jnp.sum(jnp.where(earlier & (across == down), 1.0, 0.0), axis=0, keepdims=True)
    cell = cell_ref[...].astype(jnp.float32)
    line = jnp.floor(cell / width)
    column = cell - line * width
    part = jnp.floor(column / own)
    column = column - part * own
    spot = jnp.floor((column + 0.5) / chunk)
    place = (part * chunk + (column - spot * chunk)) * rows + line
    filler = jnp.zeros((rows - 4, LANES), jnp.float32)
    meta = jnp.concatenate([place, spot, owner, rank, filler], axis=0)
    for shift in range(PLANE):
        outs[shift][outs[shift].shape[0] - 1] = meta


def keep_ends(dst, s, t, spot, value, tiles):
    if t < REACH:
        dst[s, tiles + REACH + t, spot] = pltpu.roll(value, LANES - 1, 1)
    if t >= tiles - REACH:
        dst[s, t - (tiles - REACH), spot] = pltpu.roll(value, 1, 1)


def relax_rows(src, dst, cost, count, tiles, start):
    spot = pl.ds(start, 8)
    order = sorted(range(tiles), key=lambda t: REACH <= t < tiles - REACH)
    for s in range(count):

        def load(t, shift):
            return src[s, t + REACH, pl.ds(start + shift, 8)]

        near = {t: load(t, 0) for t in range(-1, tiles + 1)}
        one = {t: jnp.minimum(load(t, -1), load(t, 1)) for t in range(-2, tiles + 2)}
        two = {t: jnp.minimum(load(t, -2), load(t, 2)) for t in range(-1, tiles + 1)}
        for t in order:
            m1 = jnp.minimum(one[t], jnp.minimum(near[t - 1], near[t + 1]))
            m2 = jnp.minimum(one[t - 1], one[t + 1])
            m5 = jnp.minimum(
                jnp.minimum(one[t - 2], one[t + 2]), jnp.minimum(two[t - 1], two[t + 1])
            )
            best = jnp.minimum(m1 + cost[0, t, spot], m2 + cost[1, t, spot])
            best = jnp.minimum(best, m5 + cost[2, t, spot])
            value = jnp.minimum(near[t], best)
            dst[s, t + REACH, spot] = value


def fill_rows(field, tiles, start):
    spot = pl.ds(start, 8)
    for s in range(field.shape[0]):
        for t in list(range(REACH)) + list(range(tiles - REACH, tiles)):
            keep_ends(field, s, t, spot, field[s, t + REACH, spot], tiles)


def fill_ends(field, tiles):
    def group(at, carry):
        for k in range(2):
            fill_rows(field, tiles, pl.multiple_of(PAD + at * 16 + k * 8, 8))
        return carry

    lax.fori_loop(0, (field.shape[2] - 3 * PAD) // 16, group, 0)


def scale_cost(cost):
    def group(at, carry):
        spot = pl.ds(pl.multiple_of(at * 8, 8), 8)
        for t in range(cost.shape[1]):
            value = cost[0, t, spot]
            cost[1, t, spot] = root_two * value
            cost[2, t, spot] = root_five * value
        return carry

    lax.fori_loop(0, cost.shape[2] // 8, group, 0)


def run_sweeps(first, second, cost, count, tiles, sweeps, groups):
    def sweep(src, dst, number):
        low = lax.shift_right_logical(number, 2)

        for step in range(sweeps // 4 + 1):

            @pl.when(low == step)
            def _():
                for at in range(step, groups - step):
                    fill_rows(dst, tiles, PAD + 8 * at - 8)
                    relax_rows(src, dst, cost, count, tiles, PAD + 8 * at)
                fill_rows(dst, tiles, PAD + 8 * (groups - step - 1))

    def pair(at, carry):
        sweep(first, second, 2 * at + 1)
        sweep(second, first, 2 * at + 2)
        return carry

    fill_ends(first, tiles)
    lax.fori_loop(0, sweeps // 2, pair, 0)


def core(field, s, tiles):
    return field.at[s, REACH : REACH + tiles]


def fence(plane, planes, halo, total, field):
    for missing, at in ((plane == 0, PAD), (plane == planes - 1, PAD + halo + total)):

        @pl.when(missing)
        def _():
            for t in range(field.shape[0]):
                field[t, at : at + halo] = jnp.full((halo, LANES), far_value, jnp.float32)


def edge_kernel(slabs, p0, p1, p2, p3, even_ref, odd_ref, sem):
    member, plane, _ = here()
    parity = lax.rem(plane, 2)
    sems = Semaphores(sem)
    copies = []
    for j, p in enumerate((p0, p1, p2, p3)):
        first, last = member == j, member == PLANE - 1 - j
        even = ((parity == 0) & last) | ((parity == 1) & first)
        odd = ((parity == 0) & first) | ((parity == 1) & last)
        copies.append((even, sems.copy(p.at[0:slabs], even_ref)))
        copies.append((odd, sems.copy(p.at[0:slabs], odd_ref)))
    run_copies(copies)


def sides(plane, halo, total):
    parity = lax.rem(plane, 2)
    above, below = PAD, PAD + halo + total
    return (
        aligned(parity * above + (1 - parity) * below),
        aligned((1 - parity) * above + parity * below),
    )


def first_kernel(count, halo, planes, edge, has_cost, *refs):
    own, (even, odd), rest = refs[0:4], refs[4:6], refs[6:]
    if has_cost:
        state, low_ref, high_ref, cost_out, one, two, cost, sem = rest
    else:
        cost_in, state, low_ref, high_ref, one, two, cost, sem = rest
    member, plane, _ = here()
    rows = own[0].shape[1]
    total = PLANE * rows
    tiles = cost.shape[1]
    sems = Semaphores(sem)
    even_at, odd_at = sides(plane, halo, total)

    def gather(slabs, field):
        copies = []
        for j in range(PLANE):
            at = aligned(PAD + halo + (member ^ j) * rows)
            copies.append(sems.copy(own[j].at[slabs], field.at[:, pl.ds(at, rows)]))
        for partner, at in ((even, even_at), (odd, odd_at)):
            copies.append(sems.copy(partner.at[slabs], field.at[:, pl.ds(at, halo)]))
        return copies

    copies = []
    for s in range(count):
        copies += gather(slice(s * tiles, (s + 1) * tiles), core(one, s, tiles))
    if has_cost:
        copies += gather(slice(count * tiles, (count + 1) * tiles), cost.at[0])
    else:
        copies.append(sems.copy(cost_in, cost))
    run_copies(copies)
    for s in range(count):
        fence(plane, planes, halo, total, core(one, s, tiles))
    if has_cost:
        fence(plane, planes, halo, total, cost.at[0])
        scale_cost(cost)
    run_sweeps(one, two, cost, count, tiles, FIRST, (total + 2 * halo) // 8)
    parity = lax.rem(plane, 2)
    top, bottom = PAD + halo, PAD + halo + total - edge
    low = aligned(parity * top + (1 - parity) * bottom)
    high = aligned((1 - parity) * top + parity * bottom)
    copies = []
    for s in range(count):
        field = core(one, s, tiles)
        slabs = slice(s * tiles, (s + 1) * tiles)
        copies.append(sems.copy(field.at[:, PAD + halo : PAD + halo + total], state.at[slabs]))
        for k in range(edge // halo):
            slabs = slice((k * count + s) * tiles, (k * count + s + 1) * tiles)
            for at, out in ((low, low_ref), (high, high_ref)):
                at = aligned(at + k * halo)
                copies.append(sems.copy(field.at[:, pl.ds(at, halo)], out.at[slabs]))
    if has_cost:
        slabs = slice(edge // halo * count * tiles, (edge // halo * count + 1) * tiles)
        for at, out in ((low + parity * halo, low_ref), (high + (1 - parity) * halo, high_ref)):
            copies.append(sems.copy(cost.at[0, :, pl.ds(aligned(at), halo)], out.at[slabs]))
    if has_cost:
        copies.append(sems.copy(cost, cost_out))
    run_copies(copies)


def last_kernel(count, sweeps, is_last, planes, state, even, odd, known, more_even, more_odd, *rest):
    if is_last:
        partial_ref, each_ref, r0, r1, r2, r3, one, two, cost, best, plain, sem = rest
    else:
        each_ref, best, one, two, cost, sem = rest
    member, plane, _ = here()
    total, part = state.shape[1], even.shape[1]
    halo = 2 * part
    rows = total // PLANE
    tiles = cost.shape[1]
    own = tiles - 1
    sems = Semaphores(sem)
    even_at, odd_at = sides(plane, halo, total)

    parity = lax.rem(plane, 2)
    copies = [
        sems.copy(
            known.at[0, :, PAD : PAD + total + 2 * part],
            cost.at[0, :, PAD + part : PAD + total + 3 * part],
        )
    ]
    slabs = slice(2 * count * tiles, (2 * count + 1) * tiles)
    for at, partner in (
        (even_at + (1 - parity) * part, more_even),
        (odd_at + parity * part, more_odd),
    ):
        copies.append(sems.copy(partner.at[slabs], cost.at[0, :, pl.ds(aligned(at), part)]))
    for s in range(count):
        field = core(one, s, tiles)
        copies.append(
            sems.copy(
                state.at[s * tiles : (s + 1) * tiles],
                field.at[:, PAD + halo : PAD + halo + total],
            )
        )
        for k in range(2):
            slabs = slice((k * count + s) * tiles, (k * count + s + 1) * tiles)
            for at, partner in ((even_at, even), (odd_at, odd)):
                at = aligned(at + k * part)
                copies.append(sems.copy(partner.at[slabs], field.at[:, pl.ds(at, part)]))
    run_copies(copies)
    for s in range(count):
        fence(plane, planes, halo, total, core(one, s, tiles))
    fence(plane, planes, halo, total, cost.at[0])
    scale_cost(cost)
    run_sweeps(one, two, cost, count, tiles, sweeps, (total + 2 * halo) // 8)

    for t in range(tiles):
        low = None
        for s in range(count):
            each = jnp.minimum(
                one[s, REACH + t, PAD + halo : PAD + halo + total], jnp.float32(clip_value)
            )
            each = each / clip_value
            each_ref[s * tiles + t] = each
            low = each if low is None else jnp.minimum(low, each)
        best[t] = jnp.minimum(low, partial_ref[t]) if is_last else low
    if not is_last:
        return
    lane = lax.broadcasted_iota(jnp.int32, (8, LANES), 1)
    orders = [((lane + (LANES - j)) * inverse(tiles)) & (LANES - 1) for j in range(tiles)]
    chosen = [lax.rem(lane + t * LANES, tiles) for t in range(own)]

    for at in range(total // 8):
        spot = slice(at * 8, at * 8 + 8)
        turned = [gather_lanes(best[j, spot], orders[j]) for j in range(tiles)]
        for t in range(own):
            value = turned[0]
            for j in range(1, tiles):
                value = jnp.where(chosen[t] == j, turned[j], value)
            plain[t, spot] = value
    run_copies(
        [
            sems.copy(plain.at[:, pl.ds(aligned((member ^ j) * rows), rows)], r)
            for j, r in enumerate((r0, r1, r2, r3))
        ]
    )


def gauge_kernel(cap, half, each_a, each_b, m0, m1, m2, m3, placed_ref, meta, sem):
    def exact(left, pick, right):
        value, found = right if left is None else left, None
        for _ in range(3):
            part = value.astype(jnp.bfloat16)
            value = value - part.astype(jnp.float32)
            pair = (pick, part) if left is None else (part, pick)
            term = jnp.dot(*pair, preferred_element_type=jnp.float32)
            found = term if found is None else found + term
        return found

    member, plane, _ = here()
    sems = Semaphores(sem)
    run_copies(
        [
            sems.copy(m.at[m.shape[0] - 1], meta.at[member ^ j])
            for j, m in enumerate((m0, m1, m2, m3))
        ]
    )
    n, sources, slots = placed_ref.shape
    rows = each_a.shape[1] // PLANE
    tiles = each_a.shape[0] // half
    height = tiles * rows
    lane = lax.broadcasted_iota(jnp.int32, (LANES, LANES), 1).astype(jnp.float32)
    place = lax.broadcasted_iota(jnp.int32, (LANES, height), 1).astype(jnp.float32)
    spot = lax.broadcasted_iota(jnp.int32, (LANES, slots), 1).astype(jnp.float32)
    device = lax.broadcasted_iota(jnp.int32, (n, LANES), 0).astype(jnp.float32)
    filler = jnp.zeros((LANES - meta.shape[1], LANES), jnp.float32)
    offset = (member * height).astype(jnp.float32)
    totals = [None] * sources
    for q in range(PLANE):
        turned = jnp.transpose(jnp.concatenate([meta[q], filler], axis=0))
        pick = jnp.where(turned[:, 0:1] - offset == place, 1.0, 0.0).astype(jnp.bfloat16)
        at_lane = turned[:, 1:2] == lane
        base = ((plane * PLANE + q) * cap).astype(jnp.float32)
        at_slot = turned[:, 3:4] + base == spot
        at_slot = jnp.where(at_slot, 1.0, 0.0).astype(jnp.bfloat16)
        blocks = []
        for s in range(sources):
            each, k = (each_a, s) if s < half else (each_b, s - half)
            block = each[k * tiles : (k + 1) * tiles, q * rows : (q + 1) * rows]
            blocks.append(block.reshape(height, LANES))
        found = exact(None, pick, jnp.concatenate(blocks, axis=1))
        values = jnp.zeros((LANES, LANES), jnp.float32)
        for s in range(sources):
            mine = jnp.where(at_lane, found[:, s * LANES : (s + 1) * LANES], 0.0)
            values = jnp.where(lane == s, jnp.sum(mine, axis=1, keepdims=True), values)
        values = jnp.transpose(values)
        to_owner = meta[q, 2:3] == device
        sent = [jnp.where(to_owner, values[s : s + 1], 0.0) for s in range(sources)]
        added = exact(jnp.concatenate(sent, axis=0), at_slot, None)
        for s in range(sources):
            term = added[s * n : (s + 1) * n]
            totals[s] = term if q == 0 else totals[s] + term
    for s in range(sources):
        placed_ref[:, s] = totals[s]


def join_kernel(r0, r1, r2, r3, gauge_ref, out_ref, result_ref):
    member, _, _ = here()
    tiles, _, _ = r0.shape
    for j, r in enumerate((r0, r1, r2, r3)):
        base = (member ^ j) * (tiles * LANES)
        for t in range(tiles):
            out_ref[:, pl.ds(pl.multiple_of(base + t * LANES, LANES), LANES)] = r[t]
    result_ref[0] = jnp.sum(gauge_ref[...], axis=0)


def shape_of(*dims):
    return jax.ShapeDtypeStruct(dims, jnp.float32)


def on_device(slowness, ocean, start_times, source_cells, gauge_cells, gauge_owner):
    axis = "space"
    n = lax.axis_size(axis)
    rows, width = slowness.shape
    sources = start_times.shape[0]
    gauges = gauge_cells.shape[0]
    planes = n // PLANE
    later_sweeps = SWEEPS * BLOCKS - FIRST
    halo, edge = 2 * FIRST, 2 * later_sweeps
    total = rows * PLANE
    tiles = width // PLANE // LANES + 1
    assert n % (2 * PLANE) == 0 and width % (PLANE * LANES) == 0 and tiles % 2 == 1
    assert gauges == LANES and sources % 2 == 0 and rows == halo
    assert 2 * SWEEPS * BLOCKS <= SIDE and edge <= total and FIRST % 2 == later_sweeps % 2 == 0
    assert edge == 2 * halo
    assert total % 16 == halo % 8 == edge % 8 == 0
    cap = max(2, 2 * gauges // n)
    half = sources // 2
    groups = (tuple(range(half)), tuple(range(half, sources)))
    size = half * tiles
    sizes = [size + tiles + 1, size]

    def call(kernel, out_shape, in_specs, out_specs, scratch, micros=2):
        return pl.pallas_call(
            kernel,
            out_shape=out_shape,
            in_specs=in_specs,
            out_specs=out_specs,
            scratch_shapes=scratch,
            compiler_params=pltpu.CompilerParams(vmem_limit_bytes=VMEM_BYTES),
            cost_estimate=pl.CostEstimate(
                flops=0, bytes_accessed=3_000_000 * micros, transcendentals=0
            ),
        )

    def vmem(*dims):
        return pltpu.VMEM(dims, jnp.float32)

    def semaphores(number):
        return pltpu.SemaphoreType.DMA((number,))

    def pack(k):
        fields = half + (k == 0)
        more = [slowness, ocean, gauge_cells.reshape(1, gauges), gauge_owner.reshape(1, gauges)]
        inputs = [source_cells, start_times] + (more if k == 0 else [])
        line = pltpu.VMEM((1, gauges), jnp.int32)
        return call(
            functools.partial(pack_kernel, groups[k], k == 0),
            [shape_of(sizes[k], rows, LANES)] * PLANE,
            [HBM] * len(inputs),
            [VMEM] * PLANE,
            [pltpu.SMEM((sources,), jnp.int32)]
            + ([line, line] if k == 0 else [])
            + [vmem(fields, rows, width)]
            + ([pltpu.VMEM((rows, width), jnp.int32)] if k == 0 else [])
            + [vmem(PLANE, fields, rows, LANES), semaphores(6)],
        )(*(pltpu.with_memory_space_constraint(x, pltpu.HBM) for x in inputs))

    def swap(x, j):
        return lax.ppermute(x, axis, [(d, d ^ j) for d in range(n)])

    def swap_planes(even, odd):
        pairs_even = [(d, (d // PLANE ^ 1) * PLANE + d % PLANE) for d in range(n)]
        pairs_odd = [
            (d, (((d // PLANE + 1) ^ 1) - 1) * PLANE + d % PLANE)
            for d in range(PLANE, n - PLANE)
        ]
        return lax.ppermute(even, axis, pairs_even), lax.ppermute(odd, axis, pairs_odd)

    pieces, beside = [], []
    for k in range(2):
        mine = pack(k)
        pieces.append([mine[0]] + [swap(mine[j], j) for j in range(1, PLANE)])
    for k in range(2):
        slabs = size + (tiles if k == 0 else 0)
        edge_call = call(
            functools.partial(edge_kernel, slabs),
            [shape_of(slabs, rows, LANES)] * 2,
            [ANY] * PLANE,
            [ANY] * 2,
            [semaphores(2 * PLANE)],
            1,
        )
        edges = edge_call(*pieces[k])
        beside.append(swap_planes(*edges))

    def buffers(deep):
        deep += 3 * PAD
        ends = tiles + 2 * REACH
        return [vmem(half, ends, deep, LANES), vmem(half, ends, deep, LANES), vmem(3, tiles, deep, LANES)]

    states, later, cost = [], [], None
    for k in range(2):
        slabs = size + (tiles if k == 0 else 0)
        scratch = buffers(total + 2 * halo)
        first_call = call(
            functools.partial(first_kernel, half, halo, planes, edge, k == 0),
            [shape_of(size, total, LANES)]
            + [shape_of(size + slabs, halo, LANES)] * 2
            + ([shape_of(*scratch[2].shape)] if k == 0 else []),
            [ANY] * (PLANE + 2 + k),
            [ANY] * (4 - k),
            scratch + [semaphores((PLANE + 2) * (half + 1) + 5 * half + 3)],
            7,
        )
        outs = first_call(*pieces[k], *beside[k], *([] if k == 0 else [cost]))
        if k == 0:
            cost = outs[3]
        states.append(outs[0])
        later.append(swap_planes(outs[1], outs[2]))

    slots = n * cap
    each, partial = [], None
    for k in range(2):
        out_shape, out_specs, more = [shape_of(size, total, LANES)], [VMEM], []
        if k == 0:
            out_shape.append(shape_of(tiles, total, LANES))
            out_specs.append(VMEM)
        else:
            out_shape += [shape_of(tiles - 1, rows, LANES)] * PLANE
            out_specs += [ANY] * PLANE
            more = [vmem(tiles, total, LANES), vmem(tiles - 1, total, LANES)]
        outs = call(
            functools.partial(last_kernel, half, later_sweeps, k == 1, planes),
            out_shape,
            [ANY] * 6 + [VMEM] * k,
            out_specs,
            buffers(total + 2 * edge) + more + [semaphores(5 * half + 3 + PLANE)],
            15,
        )(states[k], *later[k], cost, *later[0], *([] if k == 0 else [partial]))
        each.append(outs[0])
        if k == 0:
            partial = outs[1]
        else:
            returned = outs[1:]

    back = [returned[0]] + [swap(returned[j], j) for j in range(1, PLANE)]
    gauge_call = call(
        functools.partial(gauge_kernel, cap, half),
        shape_of(n, sources, slots),
        [VMEM] * 2 + [ANY] * PLANE,
        VMEM,
        [vmem(PLANE, rows, LANES), semaphores(PLANE)],
        4,
    )
    placed = gauge_call(*each, *pieces[0])
    received = lax.all_to_all(placed, axis, split_axis=0, concat_axis=0, tiled=True)
    return call(
        join_kernel,
        (shape_of(rows, width), shape_of(1, sources, slots)),
        [VMEM] * (PLANE + 1),
        (VMEM, VMEM),
        [],
    )(*back, received)


def solution(mesh):
    return jax.shard_map(
        on_device,
        mesh=mesh,
        in_specs=(
            P(("groups", "space"), None),
            P(("groups", "space"), None),
            P("groups", "space", None),
            P("groups"),
            P(("groups", "space")),
            P(("groups", "space"), None),
        ),
        out_specs=(P(("groups", "space"), None), P(("groups", "space"), None, None)),
        check_vma=False,
    )
```
